256 devices in a mesh: sec: 16 (over z, y_lo), dev: 16 (over x, y_hi, core).
Axes of the slice: x: 4, y: 4 (y_hi: 2, y_lo: 2; y = y_hi * 2 + y_lo), z: 8, core: 2. Of those that a mesh axis runs over, the one named last changes fastest.
Arguments:
- latents: float32 [16, 4, 128, 128], P('sec', None, 'dev'), may hold values from -6 to 6
- noise: float32 [6, 16, 4, 128, 128], P(None, 'sec', None, 'dev'), may hold values from -6 to 6
- rewards: float32 [16], P('sec'), may hold values from -12 to 12
- prompt_ids: int32 [16], P('sec'), may hold values from 0 to 7
- context: bfloat16 [8, 77, 2048], replicated, may hold values from -6 to 6
- time_bias: float32 [6, 640], replicated, may hold values from -6 to 6
- gain_first: float32 [640], replicated, may hold values from 0.25 to 1.75
- gain_second: float32 [640], replicated, may hold values from 0.25 to 1.75
- gain_third: float32 [640], replicated, may hold values from 0.25 to 1.75
- w_in: bfloat16 [16, 640], P('sec', 'dev'), may hold values from -1.5 to 1.5
- w_conv: bfloat16 [5760, 640], P('sec', 'dev'), may hold values from -0.078125 to 0.078125
- w_query: bfloat16 [640, 640], P('sec', 'dev'), may hold values from -0.25 to 0.25
- w_key: bfloat16 [2048, 640], P('sec', 'dev'), may hold values from -0.125 to 0.125
- w_value: bfloat16 [2048, 640], P('sec', 'dev'), may hold values from -0.125 to 0.125
- w_attn_out: bfloat16 [640, 640], P('sec', 'dev'), may hold values from -0.25 to 0.25
- w_final: float32 [640, 16], P('sec', 'dev'), may hold values from -0.25 to 0.25
- moment_first: float32 [640, 16], P('sec', 'dev'), may hold values from -6 to 6
- moment_second: float32 [640, 16], P('sec', 'dev'), may hold values from 0.05 to 5
Outputs:
- final_latents: float32 [16, 4, 128, 128], P('sec', None, 'dev')
- new_final_weight: float32 [640, 16], P('sec', 'dev')
- moment_one: float32 [640, 16], P('sec', 'dev')
- moment_two: float32 [640, 16], P('sec', 'dev')
The draws below stay inside these ranges and needn't reach their ends.
All inputs are finite; a program needn't handle non-finite values.
Results may differ from the reference program's by a relative error of at most 0.0075.
Values may be sent and summed in bfloat16 or wider, within the bound.
A program may use at most 128 MiB of HBM per device.

```python
import math
import jax
import jax.numpy as jnp
from jax import lax

C = 640
CTX = 2048
HEAD = 64
CTX_TOK = 77
FEAT = 16
LAT = 128
STEPS = 6
IMAGES = 16
NPROMPT = 8


def draw_rewards(key, part):
    position = jnp.arange(IMAGES, dtype=jnp.float32)
    scales = 1.0 + 2.0 * position / max(IMAGES - 1, 1)
    base = jax.random.normal(key, (IMAGES,), jnp.float32)
    return jnp.clip(base * scales, -12.0, 12.0)


def plant(drawn, rng, least, top_value):
    longest = drawn.shape.index(max(drawn.shape))
    spots = []
    for shift in (0, 1):
        where = [jax.random.randint(jax.random.fold_in(rng, axis), (), 0, length) for axis, length in enumerate(drawn.shape)]
        where[longest] = (where[longest] + shift) % drawn.shape[longest]
        spots.append(tuple(where))
    return drawn.at[spots[0]].set(least).at[spots[1]].set(top_value)


def shard_levels(own_key, shape, pieces, least, top_value):
    def one(dim, parts):
        heights = jax.random.uniform(jax.random.fold_in(jax.random.fold_in(own_key, 6), dim), (parts,), jnp.float32, least / len(pieces), top_value / len(pieces))
        return jnp.repeat(jnp.exp(heights), shape[dim] // parts).reshape((-1,) + (1,) * (len(shape) - dim - 1))

    loudness = one(*pieces[0])
    for cut in pieces[1:]:
        loudness = loudness * one(*cut)
    return loudness


def gaussian(stream_key, extent, width, most, pieces=(), kind=jnp.bfloat16):
    level = shard_levels(stream_key, extent, pieces, -0.22, 0.18) if pieces else 1.0
    array = jax.random.normal(stream_key, extent, jnp.float32) * width * level
    return jnp.minimum(jnp.maximum(array, -most), most).astype(kind)


def setup_inputs(seed: int = 0) -> dict:
    arg_keys = jax.random.split(jax.random.key(seed), 19)
    return {
        "latents": gaussian(arg_keys[0], (IMAGES, 4, LAT, LAT), 1.0, 6.0, ((0, 16), (2, 16)), jnp.float32),
        "noise": gaussian(arg_keys[1], (STEPS, IMAGES, 4, LAT, LAT), 1.0, 6.0, ((1, 16), (3, 16)), jnp.float32),
        "rewards": draw_rewards(jax.random.fold_in(arg_keys[18], 71), 0),
        "prompt_ids": plant(jax.random.randint(arg_keys[3], (IMAGES,), 0, NPROMPT), jax.random.fold_in(arg_keys[3], 1), 0, NPROMPT - 1).astype(jnp.int32),
        "context": gaussian(arg_keys[4], (NPROMPT, CTX_TOK, CTX), 1.0, 6.0),
        "time_bias": gaussian(arg_keys[5], (STEPS, C), 1.0, 6.0, (), jnp.float32),
        "gain_first": jnp.clip(1.0 + 0.15 * jax.random.normal(arg_keys[6], (C,), jnp.float32), 0.25, 1.75),
        "gain_second": jnp.clip(1.0 + 0.15 * jax.random.normal(arg_keys[7], (C,), jnp.float32), 0.25, 1.75),
        "gain_third": jnp.clip(1.0 + 0.15 * jax.random.normal(arg_keys[8], (C,), jnp.float32), 0.25, 1.75),
        "w_in": gaussian(arg_keys[9], (FEAT, C), FEAT ** -0.5, 1.5, ((0, 16), (1, 16))),
        "w_conv": gaussian(arg_keys[10], (9 * C, C), (9 * C) ** -0.5, 0.078125, ((0, 16), (1, 16))),
        "w_query": gaussian(arg_keys[11], (C, C), C ** -0.5, 0.25, ((0, 16), (1, 16))),
        "w_key": gaussian(arg_keys[12], (CTX, C), CTX ** -0.5, 0.125, ((0, 16), (1, 16))),
        "w_value": gaussian(arg_keys[13], (CTX, C), CTX ** -0.5, 0.125, ((0, 16), (1, 16))),
        "w_attn_out": gaussian(arg_keys[14], (C, C), C ** -0.5, 0.25, ((0, 16), (1, 16))),
        "w_final": gaussian(arg_keys[15], (C, FEAT), C ** -0.5, 0.25, ((0, 16), (1, 16)), jnp.float32),
        "moment_first": gaussian(arg_keys[16], (C, FEAT), 1.0, 6.0, ((0, 16), (1, 16)), jnp.float32),
        "moment_second": jnp.clip(jnp.exp(math.log(5.0) - 4.6051702 * jax.random.uniform(arg_keys[17], (C, FEAT), jnp.float32) ** shard_levels(arg_keys[17], (C, FEAT), ((0, 16), (1, 16)), -0.2, 0.2)), 0.05, 5.0),
    }


alpha_bars = (0.1, 0.15, 0.21, 0.28, 0.36, 0.45, 0.55)
norm_eps = 1e-06
learn_rate = 0.001

def plan(step_index):
    current = alpha_bars[step_index]
    following = alpha_bars[step_index + 1]
    sigma = math.sqrt((1.0 - following) / (1.0 - current)) * math.sqrt(1.0 - current / following)
    scale = math.sqrt(following / current)
    beta = math.sqrt(1.0 - following - sigma * sigma) - scale * math.sqrt(1.0 - current)
    return (scale, beta, sigma)

def rms_scale(values, gain):
    mean_square = lax.optimization_barrier(jnp.mean(values * values, axis=-1, keepdims=True))
    return values * lax.rsqrt(mean_square + norm_eps) * gain

def to_tokens(latent):
    batch_size, latent_chans, height, breadth = latent.shape
    blocks = latent.reshape(batch_size, latent_chans, height // 2, 2, breadth // 2, 2)
    return blocks.transpose(0, 2, 4, 1, 3, 5).reshape(batch_size, height // 2, breadth // 2, latent_chans * 4)

def from_tokens(tokens):
    batch_size, rows_here, cols_here, feature_count = tokens.shape
    blocks = tokens.reshape(batch_size, rows_here, cols_here, feature_count // 4, 2, 2)
    return blocks.transpose(0, 3, 1, 4, 2, 5).reshape(batch_size, feature_count // 4, 2 * rows_here, 2 * cols_here)

def denoise(patches, prompt_keys, prompt_values, step_bias, weights, gains):
    w_first, w_conv, w_query, w_attn_out, final_weight = weights
    batch_size, rows_here, cols_here, feature_count = patches.shape
    channels = w_first.shape[1]
    head_count = channels // HEAD
    flat_rows = batch_size * rows_here * cols_here
    hidden_in = jnp.dot(patches.astype(jnp.bfloat16).reshape(flat_rows, feature_count), w_first, preferred_element_type=jnp.float32) + step_bias
    activated = jax.nn.silu(rms_scale(hidden_in, gains[0])).astype(jnp.bfloat16).reshape(batch_size, rows_here, cols_here, channels)
    padded = jnp.pad(activated, ((0, 0), (1, 1), (1, 1), (0, 0)))
    columns = jnp.concatenate([padded[:, row_off:row_off + rows_here, col_off:col_off + cols_here] for row_off in range(3) for col_off in range(3)], axis=-1)
    mixed_rows = hidden_in + jnp.dot(columns.reshape(flat_rows, 9 * channels), w_conv, preferred_element_type=jnp.float32)
    normed = rms_scale(mixed_rows, gains[1]).astype(jnp.bfloat16)
    queries = jnp.dot(normed, w_query, preferred_element_type=jnp.float32).astype(jnp.bfloat16)
    queries = queries.reshape(batch_size, rows_here * cols_here, head_count, HEAD)
    key_heads = prompt_keys.reshape(batch_size, -1, head_count, HEAD)
    value_heads = prompt_values.reshape(batch_size, -1, head_count, HEAD)
    scores = jnp.einsum('bthd,bkhd->bthk', queries.astype(jnp.float32), key_heads.astype(jnp.float32)) / math.sqrt(HEAD)
    exponent = jnp.exp(scores)
    probabilities = (exponent / lax.optimization_barrier(jnp.sum(exponent, axis=-1, keepdims=True))).astype(jnp.bfloat16)
    attended = jnp.einsum('bthk,bkhd->bthd', probabilities.astype(jnp.float32), value_heads.astype(jnp.float32)).astype(jnp.bfloat16)
    output_rows = mixed_rows + jnp.dot(attended.reshape(flat_rows, channels), w_attn_out, preferred_element_type=jnp.float32)
    final_act = jax.nn.silu(rms_scale(output_rows, gains[2])).astype(jnp.bfloat16)
    predicted = jnp.dot(final_act, final_weight, preferred_element_type=jnp.float32)
    return (predicted.reshape(batch_size, rows_here, cols_here, feature_count), final_act)

def advantages(onehot, rewards, counts, sums, squares):
    safe_count = jnp.maximum(counts, 1.0)
    means = sums / safe_count
    spreads = jnp.sqrt(jnp.maximum(squares / safe_count - means * means, 1.0))
    own_mean = lax.optimization_barrier(jnp.sum(onehot * means[None, :], axis=1))
    own_spread = lax.optimization_barrier(jnp.sum(onehot * spreads[None, :], axis=1))
    return (rewards - own_mean) / own_spread

def reference(latents, noise, rewards, prompt_ids, context, time_bias, gain_first, gain_second, gain_third, w_in, w_conv, w_query, w_key, w_value, w_attn_out, w_final, moment_first, moment_second):
    catalog = jnp.arange(NPROMPT, dtype=jnp.int32)
    onehot = (prompt_ids[:, None] == catalog[None, :]).astype(jnp.float32)
    counts = lax.optimization_barrier(jnp.sum(onehot, axis=0))
    sums = lax.optimization_barrier(jnp.sum(onehot * rewards[:, None], axis=0))
    squares = lax.optimization_barrier(jnp.sum(onehot * (rewards * rewards)[:, None], axis=0))
    advantage = advantages(onehot, rewards, counts, sums, squares)
    flat_context = context.reshape(NPROMPT * CTX_TOK, CTX)
    all_keys = jnp.dot(flat_context, w_key, preferred_element_type=jnp.float32).astype(jnp.bfloat16).reshape(NPROMPT, CTX_TOK, C)
    all_values = jnp.dot(flat_context, w_value, preferred_element_type=jnp.float32).astype(jnp.bfloat16).reshape(NPROMPT, CTX_TOK, C)
    final_weight = w_final.astype(jnp.bfloat16)
    weights = (w_in, w_conv, w_query, w_attn_out, final_weight)
    gains = (gain_first, gain_second, gain_third)

    def one_image(item):
        latent, noise_rows, image_prompt, image_adv = item
        latent = latent[None]
        own_keys = lax.dynamic_index_in_dim(all_keys, image_prompt.astype(jnp.int32), 0, keepdims=True)
        own_values = lax.dynamic_index_in_dim(all_values, image_prompt.astype(jnp.int32), 0, keepdims=True)
        gradient = jnp.zeros((C, FEAT), jnp.float32)
        for step_index in range(STEPS):
            scale, beta, sigma = plan(step_index)
            patches = to_tokens(latent)
            predicted, final_act = denoise(patches, own_keys, own_values, time_bias[step_index], weights, gains)
            noise_now = noise_rows[step_index][None]
            noise_patch = to_tokens(noise_now).reshape(-1, FEAT)
            weighted = noise_patch * (image_adv * (beta / sigma))
            gradient = gradient + jnp.dot(final_act.astype(jnp.float32).T, weighted, precision=lax.Precision.HIGHEST)
            latent = scale * latent + beta * from_tokens(predicted) + sigma * noise_now
        return (latent[0], gradient)
    finals, grads = lax.map(one_image, (latents, noise.transpose(1, 0, 2, 3, 4), prompt_ids, advantage))
    grad_total = -lax.optimization_barrier(jnp.sum(grads, axis=0)) / IMAGES
    moment_one = 0.9 * moment_first + 0.1 * grad_total
    moment_two = 0.999 * moment_second + 0.001 * grad_total * grad_total
    new_weight = w_final - learn_rate * moment_one / (jnp.sqrt(moment_two) + 1e-08)
    return (finals, new_weight, moment_one, moment_two)
```

```python
import math

import jax
import jax.numpy as jnp
from jax import lax
from jax.experimental import pallas as pl
from jax.experimental.pallas import tpu as pltpu
from jax.sharding import PartitionSpec as P

HEAD = 64
STEPS = 6
ROWS = 4
COLS = 64
TOK = ROWS * COLS
C = 640
FEAT = 16
PAIRS = C // (2 * HEAD)
SHARD = 40
CONV_ROWS = 360
LANES = 512
FINAL_AT = 384
QUERY_AT = 400
OUT_AT = 440
IN_AT = 480
CTX_TOK = 77

alpha_bars = (0.1, 0.15, 0.21, 0.28, 0.36, 0.45, 0.55)
norm_eps = 1e-06
learn_rate = 0.001
NX, NY, NZ = 4, 4, 8
SIZE = {"x": NX, "y": NY, "z": NZ}
CLASSES = (
    ((0, 16), "yzx"),
    ((16, 32), "xzy"),
    ((32, 40), "xyz"),
)
MESH_ID = pl.DeviceIdType.MESH
F32 = jnp.float32
BF16 = jnp.bfloat16


def plan(step_index):
    current = alpha_bars[step_index]
    following = alpha_bars[step_index + 1]
    sigma = math.sqrt((1.0 - following) / (1.0 - current)) * math.sqrt(1.0 - current / following)
    scale = math.sqrt(following / current)
    beta = math.sqrt(1.0 - following - sigma * sigma) - scale * math.sqrt(1.0 - current)
    return (scale, beta, sigma)


PLANS = [plan(i) for i in range(STEPS)]


def dot(a, b):
    return jnp.dot(a, b, preferred_element_type=F32)


def dot_t(a, b):
    return lax.dot_general(a, b, (((1,), (1,)), ((), ())), preferred_element_type=F32)


def rms(values, gain):
    mean_square = jnp.mean(values * values, axis=-1, keepdims=True)
    return values * lax.rsqrt(mean_square + norm_eps) * gain


def silu(v):
    half = 0.5 * v
    return half + half * jnp.tanh(half)


def choose(index, values):
    out = jnp.float32(values[0])
    for i in range(1, len(values)):
        out = jnp.where(index == i, jnp.float32(values[i]), out)
    return out


def iota(shape, dim):
    return lax.broadcasted_iota(jnp.int32, shape, dim)


def body(
    lat_ref,
    noise_ref,
    reward_ref,
    prompt_ref,
    ctx_ref,
    bias_ref,
    g1_ref,
    g2_ref,
    g3_ref,
    w_in_ref,
    w_conv_ref,
    w_query_ref,
    w_key_ref,
    w_value_ref,
    w_out_ref,
    w_final_ref,
    m1_ref,
    m2_ref,
    x_out,
    w_new_out,
    m1_out,
    m2_out,
    G,
    KG,
    KT,
    SA,
    Wc,
    Wq,
    Wo,
    Win,
    WF,
    Kbd,
    Vbd,
    PB,
    A,
    H,
    M,
    X,
    NZT,
    NTS,
    FA,
    GA,
    GS,
    GR,
    R1,
    RR,
    g_send,
    g_recv,
    b_send,
    b_recv,
    k_send,
    k_recv,
    t_send,
    t_recv,
    h_send,
    h_recv,
    r_send,
    r_recv,
    s_send,
    s_recv,
):
    sec = lax.axis_index("sec")
    dev = lax.axis_index("dev")
    z, ylo = sec // 2, sec % 2
    xx, yhi, core = dev // 4, (dev // 2) % 2, dev % 2
    yy = yhi * 2 + ylo
    me = {"x": xx, "y": yy, "z": z}

    def device(x, y, zc, c):
        return (zc * 2 + y % 2, x * 4 + (y // 2) * 2 + c)

    def neighbour(axis, delta):
        pos = dict(me)
        pos[axis] = lax.rem(me[axis] + delta + SIZE[axis], SIZE[axis])
        return device(pos["x"], pos["y"], pos["z"], core)

    barrier = pltpu.get_barrier_semaphore()
    cross_y = (sec - 2 * ylo + 1, dev - 2 * yhi + 2 * (1 - yhi))
    for k in range(1, 16):
        pl.semaphore_signal(barrier, inc=1, device_id=(lax.rem(sec + k, 16), dev), device_id_type=MESH_ID)
        pl.semaphore_signal(barrier, inc=1, device_id=(sec, lax.rem(dev + k, 16)), device_id_type=MESH_ID)
    pl.semaphore_signal(barrier, inc=1, device_id=cross_y, device_id_type=MESH_ID)

    eye = (iota((SHARD, SHARD), 0) == iota((SHARD, SHARD), 1)).astype(BF16)
    SA[...] = jnp.zeros_like(SA)
    SA[0:CONV_ROWS, :] = w_conv_ref[...].astype(F32)
    SA[QUERY_AT : QUERY_AT + SHARD, :] = w_query_ref[...].astype(F32)
    SA[OUT_AT : OUT_AT + SHARD, :] = w_out_ref[...].astype(F32)
    SA[IN_AT : IN_AT + 1, :] = w_in_ref[...].astype(F32)
    block = dot_t(eye, SA[...].astype(BF16))
    w_fin = jnp.broadcast_to(w_final_ref[...], (SHARD, LANES))
    block = jnp.where(iota((SHARD, LANES), 1) == FINAL_AT + dev, w_fin, block)
    G[z, ylo, xx, yhi, core] = block.astype(BF16)

    KG[sec, 0:SHARD, :] = dot_t(eye, w_key_ref[...]).astype(BF16)
    KG[sec, SHARD : 2 * SHARD, :] = dot_t(eye, w_value_ref[...]).astype(BF16)
    reward = jnp.broadcast_to(reward_ref[...], (8, 128))
    prompt = jnp.broadcast_to(prompt_ref[...].astype(F32), (8, 128))
    hi = reward.astype(BF16).astype(F32)
    mid = (reward - hi).astype(BF16).astype(F32)
    low = reward - hi - mid
    lane8 = iota((8, 128), 1)
    stats = jnp.where(lane8 == 0, prompt, 0.0)
    for i, part in enumerate((hi, mid, low)):
        stats = jnp.where(lane8 == i + 1, part, stats)
    KG[sec, 80:88, :] = stats.astype(BF16)

    def turn(rows16):
        wide = jnp.concatenate([rows16, jnp.zeros((128 - FEAT, TOK), F32)], axis=0)
        return jnp.transpose(wide)

    X[...] = turn(lat_ref[...])
    PB[0, COLS : COLS + TOK, :] = X[...].astype(BF16)

    pl.semaphore_wait(barrier, 31)

    def halo_copy(t, up):
        if up:
            src, dst, to, i = PB.at[t, pl.ds(COLS, COLS)], PB.at[t, pl.ds(COLS + TOK, COLS)], dev - 1, 0
        else:
            src, dst, to, i = PB.at[t, pl.ds(TOK, COLS)], PB.at[t, pl.ds(0, COLS)], dev + 1, 1
        return pltpu.make_async_remote_copy(
            src, dst, h_send.at[t, i], h_recv.at[t, i], device_id=(sec, to), device_id_type=MESH_ID
        )

    def start_halo(t):
        @pl.when(dev > 0)
        def _():
            halo_copy(t, True).start()

        @pl.when(dev < 15)
        def _():
            halo_copy(t, False).start()

    def wait_halo(t):
        @pl.when(dev > 0)
        def _():
            halo_copy(t, True).wait_send()
            halo_copy(t, False).wait_recv()

        @pl.when(dev < 15)
        def _():
            halo_copy(t, False).wait_send()
            halo_copy(t, True).wait_recv()

    start_halo(0)

    def to_peer(src, dst, send, recv, peer):
        return pltpu.make_async_remote_copy(src, dst, send, recv, device_id=peer, device_id_type=MESH_ID)

    def key_copy(k):
        return to_peer(KG.at[sec], KG.at[sec], k_send.at[k], k_recv.at[k], (lax.rem(sec + k, 16), dev))

    for k in range(1, 16):
        key_copy(k).start()

    pushes = []

    def region(known, axis, origin, rows, half):
        index = {}
        for a in "xyz":
            if a == axis:
                index[a] = origin
            elif a in known:
                index[a] = None
            else:
                index[a] = me[a]
        lanes = pl.ds(0, LANES) if half is None else pl.ds(half * (LANES // 2), LANES // 2)
        zi = pl.ds(0, NZ) if index["z"] is None else index["z"]
        xi = pl.ds(0, NX) if index["x"] is None else index["x"]
        if index["y"] is None:
            lo_i, hi_i = pl.ds(0, 2), pl.ds(0, 2)
        else:
            lo_i, hi_i = index["y"] % 2, index["y"] // 2
        return G.at[zi, lo_i, xi, hi_i, core, pl.ds(rows[0], rows[1] - rows[0]), lanes]

    def gather(k, rows, order):
        for stage, axis in enumerate(order):
            n, known = SIZE[axis], order[:stage]
            last = stage == 2

            def copy(direction, r):
                step = 1 if direction == 0 else -1
                origin = lax.rem(me[axis] - step * (r - 1) + n, n)
                half = direction if r == n // 2 else None
                ref = region(known, axis, origin, rows, half)
                return to_peer(
                    ref, ref, g_send.at[k, stage, direction, r - 1], g_recv.at[k, stage, direction, r - 1], neighbour(axis, step)
                )

            def push(origin):
                ref = region(known, axis, lax.rem(origin + n, n), rows, None)
                i = len(pushes)
                c = to_peer(ref, ref, b_send.at[i], b_recv.at[i], (sec, dev + 1 - 2 * core))
                c.start()
                pushes.append(c)

            for r in range(1, n // 2 + 1):
                for direction in (0, 1):
                    if r > 1:
                        copy(direction, r - 1).wait_recv()
                    copy(direction, r).start()
                if last:
                    if r == 1:
                        push(me[axis])
                    else:
                        push(me[axis] - (r - 1))
                        push(me[axis] + (r - 1))
                yield
            for direction in (0, 1):
                copy(direction, n // 2).wait_recv()
            if last:
                push(me[axis] + n // 2)
            for r in range(1, n // 2 + 1):
                for direction in (0, 1):
                    copy(direction, r).wait_send()

    def keys_and_values():
        for k in range(1, 16):
            key_copy(k).wait()
        yield
        wide = jnp.concatenate([KG[s, 0:80, :] for s in range(16)], axis=1)
        own = dot_t(wide, ctx_ref[...])
        KT[dev] = jnp.zeros_like(KT[dev])
        KT[dev, :, 0:80] = own.astype(BF16)

        def copy(k):
            return to_peer(KT.at[dev], KT.at[dev], t_send.at[k], t_recv.at[k], (sec, lax.rem(dev + k, 16)))

        for k in range(1, 16):
            copy(k).start()
        yield
        yield
        yield
        for k in range(1, 16):
            copy(k).wait()
        kt = jnp.concatenate([KT[d, 0:SHARD, :] for d in range(16)], axis=0)
        vt = jnp.concatenate([KT[d, SHARD : 2 * SHARD, :] for d in range(16)], axis=0)
        v = jnp.transpose(vt.astype(F32))
        row = iota((128, 128), 0)
        lane = iota((128, 128), 1)
        for p in range(PAIRS):
            part = kt[128 * p : 128 * (p + 1), :].astype(F32) * (1.0 / math.sqrt(HEAD))
            Kbd[p, :, 0:128] = jnp.where(row < HEAD, part, 0.0).astype(BF16)
            Kbd[p, :, 128:256] = jnp.where(row < HEAD, 0.0, part).astype(BF16)
            part = v[:, 128 * p : 128 * (p + 1)]
            Vbd[p, 0:128, :] = jnp.where(lane < HEAD, part, 0.0).astype(BF16)
            Vbd[p, 128:256, :] = jnp.where(lane < HEAD, 0.0, part).astype(BF16)

    def split_noise():
        for t in range(STEPS):
            nt = noise_ref[t]
            NZT[t] = turn(nt)
            top = nt.astype(BF16)
            NTS[t, 0:FEAT, :] = top
            NTS[t, FEAT : 2 * FEAT, :] = (nt - top.astype(F32)).astype(BF16)
        yield

    running = [gather(k, rows, order) for k, (rows, order) in enumerate(CLASSES)]
    running += [keys_and_values(), split_noise()]
    while running:
        left = []
        for g in running:
            try:
                next(g)
                left.append(g)
            except StopIteration:
                pass
        running = left
    for c in pushes:
        c.wait()

    Win[...] = jnp.zeros_like(Win)
    lane_w = iota((SHARD, 128), 1)

    def settle(zi, carry):
        turned = []
        for lo in range(2):
            parts = G[zi, lo].astype(F32)
            flat = parts.reshape(C, LANES)
            tail = jnp.sum(parts.reshape(16, SHARD, LANES)[:, :, FINAL_AT:LANES], axis=0)
            WF[zi, lo] = jnp.where(lane_w < FEAT, tail, 0.0)
            turned.append(jnp.transpose(flat))
        conv = jnp.concatenate([w[0:CONV_ROWS] for w in turned], axis=0).astype(BF16)
        Wc[pl.ds(pl.multiple_of(zi * 2 * CONV_ROWS, 16), 2 * CONV_ROWS), :] = conv
        at = pl.ds(pl.multiple_of(zi * 2 * SHARD, 16), 2 * SHARD)
        Wq[at, :] = jnp.concatenate([w[QUERY_AT : QUERY_AT + SHARD] for w in turned], axis=0).astype(BF16)
        Wo[at, :] = jnp.concatenate([w[OUT_AT : OUT_AT + SHARD] for w in turned], axis=0).astype(BF16)
        for lo in range(2):
            Win[pl.ds(zi * 2 + lo, 1), :] = turned[lo][IN_AT : IN_AT + 1]
        return carry

    lax.fori_loop(0, NZ, settle, 0)

    token_col = iota((TOK, C), 0) % COLS
    tok_row = iota((2 * HEAD * 2, 2 * HEAD * 2), 0)
    tok_col = iota((2 * HEAD * 2, 2 * HEAD * 2), 1)
    ones = (((tok_row < 128) == (tok_col < 128)) & (tok_row % 128 < CTX_TOK)).astype(BF16)
    GA[...] = jnp.zeros_like(GA)

    def spread(act, at, n):
        col = iota((n, C), 0) % COLS
        rows = pl.ds(at, n)
        A[rows, C : 2 * C] = act.astype(BF16)
        A[rows, 0:C] = jnp.where(col == 0, 0.0, pltpu.roll(act, 1, 0)).astype(BF16)
        A[rows, 2 * C : 3 * C] = jnp.where(col == COLS - 1, 0.0, pltpu.roll(act, n - 1, 0)).astype(BF16)

    def denoise(t, carry):
        scale = choose(t, [p[0] for p in PLANS])
        beta = choose(t, [p[1] for p in PLANS])
        sigma = choose(t, [p[2] for p in PLANS])
        weight = choose(t, [p[1] / p[2] for p in PLANS])
        bias = bias_ref[pl.ds(t, 1), :]
        w_first = Win[...].astype(BF16)
        hidden = dot(PB[t, COLS : COLS + TOK, :], w_first) + bias
        H[...] = hidden
        spread(silu(rms(hidden, g1_ref[...])), COLS, TOK)
        M[...] = H[...] + dot(A[COLS : COLS + TOK, :], Wc[3 * C : 6 * C, :])
        wait_halo(t)
        edge = jnp.concatenate([PB[t, 0:COLS, :], PB[t, COLS + TOK :, :]], axis=0)
        act = silu(rms(dot(edge, w_first) + bias, g1_ref[...]))
        above = jnp.where(dev > 0, act[0:COLS], 0.0)
        below = jnp.where(dev < 15, act[COLS:], 0.0)
        spread(above, 0, COLS)
        spread(below, COLS + TOK, COLS)
        M[...] += dot(A[0:TOK, :], Wc[0 : 3 * C, :])
        M[...] += dot(A[2 * COLS : 2 * COLS + TOK, :], Wc[6 * C : 9 * C, :])

        def finish(ranges):
            def load(ref, *lead):
                return jnp.concatenate([ref[(*lead, slice(a, b))] for a, b in ranges], axis=0)

            mixed = load(M)
            normed = rms(mixed, g2_ref[...]).astype(BF16)
            queries = dot(normed, Wq[...]).astype(BF16)
            heads = []
            for p in range(PAIRS):
                e = jnp.exp(dot(queries[:, 128 * p : 128 * (p + 1)], Kbd[p]))
                total = dot(e.astype(BF16), ones)
                heads.append(dot((e * (1.0 / total)).astype(BF16), Vbd[p]).astype(BF16))
            out = mixed + dot(jnp.concatenate(heads, axis=1), Wo[...])
            final = silu(rms(out, g3_ref[...])).astype(BF16)
            w_last = WF[...].reshape(C, 128).astype(BF16)
            x_new = scale * load(X) + beta * dot(final, w_last) + sigma * load(NZT, t)
            at = 0
            for a, b in ranges:
                n = b - a
                FA[a:b, :] = final[at : at + n]
                X[a:b, :] = x_new[at : at + n]
                PB[t + 1, a + COLS : b + COLS, :] = x_new[at : at + n].astype(BF16)
                at += n

        finish(((0, COLS), (TOK - COLS, TOK)))

        @pl.when(t < STEPS - 1)
        def _():
            start_halo(t + 1)

        finish(((COLS, TOK - COLS),))
        GA[...] += weight * dot(NTS[t], FA[...])
        return carry

    lax.fori_loop(0, STEPS, denoise, 0)

    x_out[...] = jnp.transpose(X[...])[0:FEAT]

    table = jnp.concatenate([KG[s, 80:88, :].astype(F32)[0:1] for s in range(16)], axis=0)
    ids = table[:, 0:1]
    rewards = table[:, 1:2] + table[:, 2:3] + table[:, 3:4]
    same = jnp.where(ids == prompt_ref[...].astype(F32), 1.0, 0.0)
    count = jnp.maximum(jnp.sum(same, axis=0, keepdims=True), 1.0)
    mean = jnp.sum(same * rewards, axis=0, keepdims=True) / count
    square = jnp.sum(same * (rewards * rewards), axis=0, keepdims=True) / count
    spread_1 = jnp.sqrt(jnp.maximum(square - mean * mean, 1.0))
    advantage = (reward_ref[...] - mean) / spread_1

    grad = (GA[0:FEAT, :] + GA[FEAT : 2 * FEAT, :]) * (advantage * (-1.0 / 16.0))
    GS[...] = jnp.zeros_like(GS)
    for j in range(5):
        GS[:, j, :] = grad[:, 128 * j : 128 * (j + 1)]

    def column_copy(k):
        peer = lax.rem(dev + k, 16)
        return to_peer(GS.at[peer], GR.at[dev], r_send.at[k], r_recv.at[k], (sec, peer))

    for k in range(1, 16):
        column_copy(k).start()
    GR[dev] = GS[dev]
    for k in range(1, 16):
        column_copy(k).wait()
    R1[...] = jnp.sum(GR[...], axis=0)

    def row_copy(k):
        return to_peer(R1, RR.at[sec], s_send.at[k], s_recv.at[k], (lax.rem(sec + k, 16), dev))

    for k in range(1, 16):
        row_copy(k).start()
    RR[sec] = R1[...]
    for k in range(1, 16):
        row_copy(k).wait()
    total = jnp.sum(RR[...], axis=0)
    picked = jnp.zeros((SHARD, 128), F32)
    want = iota((SHARD, 128), 0) + sec * SHARD
    for j in range(5):
        picked = jnp.where(iota((SHARD, 128), 1) + 128 * j == want, jnp.broadcast_to(total[j : j + 1], (SHARD, 128)), picked)
    g = jnp.sum(picked, axis=1, keepdims=True)
    m1 = 0.9 * m1_ref[...] + 0.1 * g
    m2 = 0.999 * m2_ref[...] + 0.001 * g * g
    m1_out[...] = m1
    m2_out[...] = m2
    w_new_out[...] = w_final_ref[...] - learn_rate * m1 / (jnp.sqrt(m2) + 1e-08)


def to_features(latent):
    lead = latent.shape[0]
    blocks = latent.reshape(lead, 4, ROWS, 2, COLS, 2)
    return blocks.transpose(0, 1, 3, 5, 2, 4).reshape(lead, FEAT, TOK)


def per_device(
    latents,
    noise,
    rewards,
    prompt_ids,
    context,
    time_bias,
    gain_first,
    gain_second,
    gain_third,
    w_in,
    w_conv,
    w_query,
    w_key,
    w_value,
    w_attn_out,
    w_final,
    moment_first,
    moment_second,
):
    lat = to_features(latents)[0]
    noi = to_features(noise.reshape(STEPS, 4, 2 * ROWS, 2 * COLS))
    own = lax.dynamic_index_in_dim(context, prompt_ids[0], 0, keepdims=False)
    own = jnp.pad(own, ((0, 3), (0, 0)))
    vmem = pl.BlockSpec(memory_space=pltpu.VMEM)
    small = jax.ShapeDtypeStruct((SHARD, 1), F32)
    dma = pltpu.SemaphoreType.DMA
    x_new, w_new, m1, m2 = pl.pallas_call(
        body,
        out_shape=(jax.ShapeDtypeStruct((FEAT, TOK), F32), small, small, small),
        in_specs=[vmem] * 18,
        out_specs=(vmem,) * 4,
        scratch_shapes=[
            pltpu.VMEM((NZ, 2, NX, 2, 2, SHARD, LANES), BF16),
            pltpu.VMEM((16, 88, 128), BF16),
            pltpu.VMEM((16, 80, 128), BF16),
            pltpu.VMEM((LANES, SHARD), F32),
            pltpu.VMEM((9 * C, C), BF16),
            pltpu.VMEM((C, C), BF16),
            pltpu.VMEM((C, C), BF16),
            pltpu.VMEM((128, C), F32),
            pltpu.VMEM((NZ, 2, SHARD, 128), F32),
            pltpu.VMEM((PAIRS, 128, 256), BF16),
            pltpu.VMEM((PAIRS, 256, 128), BF16),
            pltpu.VMEM((STEPS + 1, TOK + 2 * COLS, 128), BF16),
            pltpu.VMEM((TOK + 2 * COLS, 3 * C), BF16),
            pltpu.VMEM((TOK, C), F32),
            pltpu.VMEM((TOK, C), F32),
            pltpu.VMEM((TOK, 128), F32),
            pltpu.VMEM((STEPS, TOK, 128), F32),
            pltpu.VMEM((STEPS, 2 * FEAT, TOK), BF16),
            pltpu.VMEM((TOK, C), BF16),
            pltpu.VMEM((2 * FEAT, C), F32),
            pltpu.VMEM((16, 8, 128), F32),
            pltpu.VMEM((16, 8, 128), F32),
            pltpu.VMEM((8, 128), F32),
            pltpu.VMEM((16, 8, 128), F32),
            dma((3, 3, 2, 4)),
            dma((3, 3, 2, 4)),
            dma((16,)),
            dma((16,)),
            dma((16,)),
            dma((16,)),
            dma((16,)),
            dma((16,)),
            dma((STEPS, 2)),
            dma((STEPS, 2)),
            dma((16,)),
            dma((16,)),
            dma((16,)),
            dma((16,)),
        ],
        compiler_params=pltpu.CompilerParams(
            collective_id=0, has_side_effects=True, vmem_limit_bytes=58 * 1024 * 1024
        ),
        name="ddpo",
    )(
        lat,
        noi,
        rewards.reshape(1, 1),
        prompt_ids.reshape(1, 1),
        own,
        time_bias,
        gain_first.reshape(1, C),
        gain_second.reshape(1, C),
        gain_third.reshape(1, C),
        w_in,
        w_conv,
        w_query,
        w_key,
        w_value,
        w_attn_out,
        w_final,
        moment_first,
        moment_second,
    )
    blocks = x_new.reshape(4, 2, 2, ROWS, COLS)
    latent = blocks.transpose(0, 3, 1, 4, 2).reshape(1, 4, 2 * ROWS, 2 * COLS)
    return (latent, w_new, m1, m2)


def solution(mesh):
    placed = (
        P("sec", None, "dev", None),
        P(None, "sec", None, "dev", None),
        P("sec"),
        P("sec"),
        P(),
        P(),
        P(),
        P(),
        P(),
        P("sec", "dev"),
        P("sec", "dev"),
        P("sec", "dev"),
        P("sec", "dev"),
        P("sec", "dev"),
        P("sec", "dev"),
        P("sec", "dev"),
        P("sec", "dev"),
        P("sec", "dev"),
    )
    return jax.shard_map(
        per_device,
        mesh=mesh,
        in_specs=placed,
        out_specs=(P("sec", None, "dev", None), P("sec", "dev"), P("sec", "dev"), P("sec", "dev")),
        check_vma=False,
    )
```

```python
import math

import jax
import jax.numpy as jnp
from jax import lax
from jax.experimental import pallas as pl
from jax.experimental.pallas import tpu as pltpu
from jax.sharding import PartitionSpec as P

HEAD = 64
STEPS = 6
ROWS = 4
COLS = 64
TOK = ROWS * COLS
C = 640
FEAT = 16
PAIRS = C // (2 * HEAD)
SHARD = 40
CONV_ROWS = 360
LANES = 512
FINAL_AT = 384
QUERY_AT = 400
OUT_AT = 440
IN_AT = 480
CTX_TOK = 77

alpha_bars = (0.1, 0.15, 0.21, 0.28, 0.36, 0.45, 0.55)
norm_eps = 1e-06
learn_rate = 0.001
NX, NY, NZ = 4, 4, 8
SIZE = {"x": NX, "y": NY, "z": NZ}
CLASSES = (
    ((0, 16), "zyx"),
    ((16, 32), "zxy"),
    ((32, 40), "xyz"),
)
MESH_ID = pl.DeviceIdType.MESH
F32 = jnp.float32
BF16 = jnp.bfloat16


def plan(step_index):
    current = alpha_bars[step_index]
    following = alpha_bars[step_index + 1]
    sigma = math.sqrt((1.0 - following) / (1.0 - current)) * math.sqrt(1.0 - current / following)
    scale = math.sqrt(following / current)
    beta = math.sqrt(1.0 - following - sigma * sigma) - scale * math.sqrt(1.0 - current)
    return (scale, beta, sigma)


PLANS = [plan(i) for i in range(STEPS)]


def dot(a, b):
    return jnp.dot(a, b, preferred_element_type=F32)


def dot_t(a, b):
    return lax.dot_general(a, b, (((1,), (1,)), ((), ())), preferred_element_type=F32)


def rms(values, gain):
    mean_square = jnp.mean(values * values, axis=-1, keepdims=True)
    return values * lax.rsqrt(mean_square + norm_eps) * gain


def silu(v):
    half = 0.5 * v
    return half + half * jnp.tanh(half)


def choose(index, values):
    out = jnp.float32(values[0])
    for i in range(1, len(values)):
        out = jnp.where(index == i, jnp.float32(values[i]), out)
    return out


def iota(shape, dim):
    return lax.broadcasted_iota(jnp.int32, shape, dim)


def body(
    lat_ref,
    noise_ref,
    reward_ref,
    prompt_ref,
    ctx_ref,
    bias_ref,
    g1_ref,
    g2_ref,
    g3_ref,
    w_in_ref,
    w_conv_ref,
    w_query_ref,
    w_key_ref,
    w_value_ref,
    w_out_ref,
    w_final_ref,
    x_out,
    g_out,
    CX,
    G,
    KG,
    KT,
    Wc,
    Wq,
    Wo,
    Win,
    WS,
    WF,
    WI,
    Kbd,
    Vbd,
    PB,
    A,
    H,
    M,
    X,
    NZT,
    NTS,
    FA,
    GA,
    GS,
    GR,
    R1,
    RR,
    a_send,
    a_recv,
    l_send,
    l_recv,
    g_send,
    g_recv,
    b_send,
    b_recv,
    k_send,
    k_recv,
    t_send,
    t_recv,
    h_send,
    h_recv,
    r_send,
    r_recv,
    s_send,
    s_recv,
    c_sem,
):
    sec = lax.axis_index("sec")
    dev = lax.axis_index("dev")
    z, ylo = sec // 2, sec % 2
    xx, yhi, core = dev // 4, (dev // 2) % 2, dev % 2
    yy = yhi * 2 + ylo
    me = {"x": xx, "y": yy, "z": z}

    def device(x, y, zc, c):
        return (zc * 2 + y % 2, x * 4 + (y // 2) * 2 + c)

    def neighbour(axis, delta):
        pos = dict(me)
        pos[axis] = lax.rem(me[axis] + delta + SIZE[axis], SIZE[axis])
        return device(pos["x"], pos["y"], pos["z"], core)

    barrier = pltpu.get_barrier_semaphore()
    cross_y = (sec - 2 * ylo + 1, dev - 2 * yhi + 2 * (1 - yhi))
    for k in range(1, 16):
        pl.semaphore_signal(barrier, inc=1, device_id=(lax.rem(sec + k, 16), dev), device_id_type=MESH_ID)
        pl.semaphore_signal(barrier, inc=1, device_id=(sec, lax.rem(dev + k, 16)), device_id_type=MESH_ID)
    pl.semaphore_signal(barrier, inc=1, device_id=cross_y, device_id_type=MESH_ID)

    context_copy = pltpu.make_async_copy(ctx_ref, CX, c_sem)
    context_copy.start()

    eye = (iota((SHARD, SHARD), 0) == iota((SHARD, SHARD), 1)).astype(BF16)
    lane40 = iota((SHARD, 128), 1)
    row40 = iota((SHARD, 128), 0)

    def place(square, at):
        turned = dot_t(eye, square).astype(BF16)
        return dot(turned, (lane40 == row40 + (at - FINAL_AT)).astype(BF16))

    def stand(row):
        wide = jnp.broadcast_to(row.astype(F32), (SHARD, SHARD))
        on_diagonal = iota((SHARD, SHARD), 0) == iota((SHARD, SHARD), 1)
        return jnp.sum(jnp.where(on_diagonal, wide, 0.0), axis=1, keepdims=True)

    tail = place(w_query_ref[...], QUERY_AT) + place(w_out_ref[...], OUT_AT)
    tail = jnp.where(lane40 == IN_AT - FINAL_AT, stand(w_in_ref[...]), tail)
    tail = jnp.where(lane40 == dev, stand(w_final_ref[...]), tail)
    G[z, ylo, xx, yhi, core, :, 256:FINAL_AT] = jnp.zeros((SHARD, 128), BF16)
    G[z, ylo, xx, yhi, core, :, 0:CONV_ROWS] = w_conv_ref[...]
    G[z, ylo, xx, yhi, core, :, FINAL_AT:LANES] = tail.astype(BF16)

    pick = iota((128, 128), 1) == 2 * (iota((128, 128), 0) % COLS) + iota((128, 128), 0) // COLS
    pick = pick.astype(BF16)

    def split(v):
        top = v.astype(BF16)
        rest = v - top.astype(F32)
        mid = rest.astype(BF16)
        return top, mid, (rest - mid.astype(F32)).astype(BF16)

    own_row = iota((TOK, 2 * 32), 0) // COLS == (iota((TOK, 2 * 32), 1) % 8) // 2

    def turn(rows32):
        cols = sum(dot_t(pick, part) for part in split(rows32))
        both = jnp.concatenate([cols[0:COLS], cols[COLS : 2 * COLS]], axis=1)
        return jnp.where(own_row, jnp.concatenate([both] * ROWS, axis=0), 0.0)

    pl.semaphore_wait(barrier, 31)

    def halo_copy(t, up):
        if up:
            src, dst, to, i = PB.at[t, pl.ds(COLS, COLS)], PB.at[t, pl.ds(COLS + TOK, COLS)], dev - 1, 0
        else:
            src, dst, to, i = PB.at[t, pl.ds(TOK, COLS)], PB.at[t, pl.ds(0, COLS)], dev + 1, 1
        return pltpu.make_async_remote_copy(
            src, dst, h_send.at[t, i], h_recv.at[t, i], device_id=(sec, to), device_id_type=MESH_ID
        )

    def start_halo(t):
        @pl.when(dev > 0)
        def _():
            halo_copy(t, True).start()

        @pl.when(dev < 15)
        def _():
            halo_copy(t, False).start()

    def wait_halo(t):
        @pl.when(dev > 0)
        def _():
            halo_copy(t, True).wait_send()
            halo_copy(t, False).wait_recv()

        @pl.when(dev < 15)
        def _():
            halo_copy(t, False).wait_send()
            halo_copy(t, True).wait_recv()

    def to_peer(src, dst, send, recv, peer):
        return pltpu.make_async_remote_copy(src, dst, send, recv, device_id=peer, device_id_type=MESH_ID)

    def key_copy(k):
        return to_peer(KG.at[sec], KG.at[sec], k_send.at[k], k_recv.at[k], (lax.rem(sec + k, 16), dev))

    sent = []
    pushes = []

    def region(rows, half, **where):
        zi, xi = where["z"], where["x"]
        zi = pl.ds(0, NZ) if zi is None else zi
        xi = pl.ds(0, NX) if xi is None else xi
        if where["y"] is None:
            lo_i, hi_i = pl.ds(0, 2), pl.ds(0, 2)
        else:
            lo_i, hi_i = where["y"] % 2, where["y"] // 2
        lanes = pl.ds(0, LANES) if half is None else pl.ds(half * (LANES // 2), LANES // 2)
        return G.at[zi, lo_i, xi, hi_i, core, pl.ds(rows[0], rows[1] - rows[0]), lanes]

    def along(axis, delta):
        return lax.rem(me[axis] + delta + SIZE[axis], SIZE[axis])

    def gather(k, rows, order):
        first, second, third = order
        n = SIZE[third]

        def block_copy(j):
            ref = region(rows, None, **me)
            return to_peer(ref, ref, a_send.at[k, j], a_recv.at[k, j], neighbour(first, j))

        def line_copy(j):
            ref = region(rows, None, **{first: None, second: me[second], third: me[third]})
            return to_peer(ref, ref, l_send.at[k, j], l_recv.at[k, j], neighbour(second, j))

        def ring_copy(j, direction, r):
            step = 1 if direction == 0 else -1
            half = direction if r == n // 2 else None
            place_ = {first: None, second: along(second, -j), third: along(third, -step * (r - 1))}
            ref = region(rows, half, **place_)
            return to_peer(
                ref, ref, g_send.at[k, j, direction, r - 1], g_recv.at[k, j, direction, r - 1], neighbour(third, step)
            )

        def push(j, delta):
            place_ = {first: None, second: None if j is None else along(second, -j), third: along(third, delta)}
            ref = region(rows, None, **place_)
            i = len(pushes)
            c = to_peer(ref, ref, b_send.at[i], b_recv.at[i], (sec, dev + 1 - 2 * core))
            c.start()
            pushes.append(c)

        def start(c):
            c.start()
            sent.append(c)

        for j in range(1, SIZE[first]):
            start(block_copy(j))
        yield
        for j in range(1, SIZE[first]):
            block_copy(j).wait_recv()
        for j in (1, 3, 2):
            start(line_copy(j))
        for direction in (0, 1):
            start(ring_copy(0, direction, 1))
        yield
        for j in (1, 3, 2):
            line_copy(j).wait_recv()
            for direction in (0, 1):
                start(ring_copy(j, direction, 1))
            yield
        push(None, 0)
        for r in range(2, n // 2 + 1):
            for j in (0, 1, 3, 2):
                for direction in (0, 1):
                    ring_copy(j, direction, r - 1).wait_recv()
                    start(ring_copy(j, direction, r))
                yield
            push(None, r - 1)
            push(None, -(r - 1))
        for j in (0, 1, 3, 2):
            for direction in (0, 1):
                ring_copy(j, direction, n // 2).wait_recv()
            push(j, n // 2)
            yield

    def keys_and_values():
        KG[sec, 0:SHARD, :] = w_key_ref[...]
        KG[sec, SHARD : 2 * SHARD, :] = w_value_ref[...]
        reward = jnp.broadcast_to(reward_ref[...], (8, 128))
        prompt = jnp.broadcast_to(prompt_ref[...].astype(F32), (8, 128))
        hi = reward.astype(BF16).astype(F32)
        mid = (reward - hi).astype(BF16).astype(F32)
        low = reward - hi - mid
        lane8 = iota((8, 128), 1)
        stats = jnp.where(lane8 == 0, prompt, 0.0)
        for i, part in enumerate((hi, mid, low)):
            stats = jnp.where(lane8 == i + 1, part, stats)
        KG[sec, 80:88, :] = stats.astype(BF16)
        yield
        yield
        for k in range(1, 16):
            key_copy(k).start()
        yield
        yield
        yield
        yield
        yield
        yield
        for k in range(1, 16):
            key_copy(k).wait()
        wide = jnp.concatenate([KG[s, 0:80, :] for s in range(16)], axis=1)
        context_copy.wait()
        every = dot_t(wide, CX[...]).astype(BF16)
        n = CX.shape[0]
        mine = iota((n, 128), 0) == 8 * iota((n, 128), 1) + prompt_ref[...]
        KT[dev] = dot(every, mine.astype(BF16)).astype(BF16)

        def copy(k):
            return to_peer(KT.at[dev], KT.at[dev], t_send.at[k], t_recv.at[k], (sec, lax.rem(dev + k, 16)))

        for k in range(1, 16):
            copy(k).start()
        yield
        yield
        yield
        yield
        yield
        yield
        for k in range(1, 16):
            copy(k).wait()
        kt = jnp.concatenate([KT[d, 0:SHARD, :] for d in range(16)], axis=0)
        vt = jnp.concatenate([KT[d, SHARD : 2 * SHARD, :] for d in range(16)], axis=0)
        v = jnp.transpose(vt.astype(F32))
        row = iota((128, 128), 0)
        lane = iota((128, 128), 1)
        for p in range(PAIRS):
            part = kt[128 * p : 128 * (p + 1), :].astype(F32) * (1.0 / math.sqrt(HEAD))
            Kbd[p, :, 0:128] = jnp.where(row < HEAD, part, 0.0).astype(BF16)
            Kbd[p, :, 128:256] = jnp.where(row < HEAD, 0.0, part).astype(BF16)
            part = v[:, 128 * p : 128 * (p + 1)]
            Vbd[p, 0:128, :] = jnp.where(lane < HEAD, part, 0.0).astype(BF16)
            Vbd[p, 128:256, :] = jnp.where(lane < HEAD, 0.0, part).astype(BF16)

    def tokens():
        X[...] = jnp.zeros_like(X)
        X[:, 0:64] = turn(lat_ref[...])
        PB[0, COLS : COLS + TOK, :] = X[...].astype(BF16)
        start_halo(0)
        yield
        yield
        GA[...] = jnp.zeros_like(GA)
        GS[...] = jnp.zeros_like(GS)
        Win[...] = jnp.zeros_like(Win)
        for t in range(STEPS):
            yield
            yield
            nt = turn(noise_ref[32 * t : 32 * (t + 1), :])
            NZT[t] = jnp.concatenate([nt, jnp.zeros_like(nt)], axis=1)
            top = nt.astype(BF16).astype(F32)
            NTS[t] = jnp.transpose(jnp.concatenate([top, nt - top], axis=1)).astype(BF16)

    running = [gather(k, rows, order) for k, (rows, order) in enumerate(CLASSES)]
    running += [keys_and_values(), tokens()]
    while running:
        left = []
        for g in running:
            try:
                next(g)
                left.append(g)
            except StopIteration:
                pass
        running = left
    for c in sent:
        c.wait_send()
    for c in pushes:
        c.wait()

    lane_w = iota((SHARD, 128), 1)

    def settle(zi, carry):
        turned = []
        for lo in range(2):
            parts = G[zi, lo].astype(F32)
            flat = parts.reshape(C, LANES)
            tail = jnp.sum(parts.reshape(16, SHARD, LANES)[:, :, FINAL_AT:LANES], axis=0)
            WS[zi, lo] = jnp.where(lane_w < FEAT, tail, 0.0)
            turned.append(jnp.transpose(flat))
        conv = jnp.concatenate([w[0:CONV_ROWS] for w in turned], axis=0).astype(BF16)
        Wc[pl.ds(pl.multiple_of(zi * 2 * CONV_ROWS, 16), 2 * CONV_ROWS), :] = conv
        at = pl.ds(pl.multiple_of(zi * 2 * SHARD, 16), 2 * SHARD)
        Wq[at, :] = jnp.concatenate([w[QUERY_AT : QUERY_AT + SHARD] for w in turned], axis=0).astype(BF16)
        Wo[at, :] = jnp.concatenate([w[OUT_AT : OUT_AT + SHARD] for w in turned], axis=0).astype(BF16)
        for lo in range(2):
            Win[pl.ds(zi * 2 + lo, 1), :] = turned[lo][IN_AT : IN_AT + 1]
        return carry

    lax.fori_loop(0, NZ, settle, 0)

    def spread_of(lane, feature):
        return (lane < 64) & (feature == ((lane // 8) % 4) * 4 + (lane % 2) * 2 + lane // 32)

    by_col = spread_of(iota((128, 128), 1), iota((128, 128), 0)).astype(BF16)
    by_row = spread_of(iota((128, 128), 0), iota((128, 128), 1)).astype(BF16)
    WF[...] = dot(WS[...].reshape(C, 128).astype(BF16), by_col).astype(BF16)
    WI[...] = dot(by_row, Win[...].astype(BF16)).astype(BF16)
    valid = iota((TOK, 128), 0) // COLS == (iota((TOK, 128), 1) % 8) // 2

    token_col = iota((TOK, C), 0) % COLS
    tok_row = iota((2 * HEAD * 2, 2 * HEAD * 2), 0)
    tok_col = iota((2 * HEAD * 2, 2 * HEAD * 2), 1)
    ones = (((tok_row < 128) == (tok_col < 128)) & (tok_row % 128 < CTX_TOK)).astype(BF16)

    def spread(act, at, n):
        col = iota((n, C), 0) % COLS
        rows = pl.ds(at, n)
        A[rows, C : 2 * C] = act.astype(BF16)
        A[rows, 0:C] = jnp.where(col == 0, 0.0, pltpu.roll(act, 1, 0)).astype(BF16)
        A[rows, 2 * C : 3 * C] = jnp.where(col == COLS - 1, 0.0, pltpu.roll(act, n - 1, 0)).astype(BF16)

    def denoise(t, carry):
        scale = choose(t, [p[0] for p in PLANS])
        beta = choose(t, [p[1] for p in PLANS])
        sigma = choose(t, [p[2] for p in PLANS])
        weight = choose(t, [p[1] / p[2] for p in PLANS])
        bias = bias_ref[pl.ds(t, 1), :]
        w_first = WI[...]
        hidden = dot(PB[t, COLS : COLS + TOK, :], w_first) + bias
        H[...] = hidden
        spread(silu(rms(hidden, g1_ref[...].reshape(1, C))), COLS, TOK)
        M[...] = H[...] + dot(A[COLS : COLS + TOK, :], Wc[3 * C : 6 * C, :])
        wait_halo(t)
        edge = jnp.concatenate([PB[t, 0:COLS, :], PB[t, COLS + TOK :, :]], axis=0)
        act = silu(rms(dot(edge, w_first) + bias, g1_ref[...].reshape(1, C)))
        above = jnp.where(dev > 0, act[0:COLS], 0.0)
        below = jnp.where(dev < 15, act[COLS:], 0.0)
        spread(above, 0, COLS)
        spread(below, COLS + TOK, COLS)
        M[...] += dot(A[0:TOK, :], Wc[0 : 3 * C, :])
        M[...] += dot(A[2 * COLS : 2 * COLS + TOK, :], Wc[6 * C : 9 * C, :])

        def finish(ranges):
            def load(ref, *lead):
                return jnp.concatenate([ref[(*lead, slice(a, b))] for a, b in ranges], axis=0)

            mixed = load(M)
            normed = rms(mixed, g2_ref[...].reshape(1, C)).astype(BF16)
            queries = dot(normed, Wq[...]).astype(BF16)
            heads = []
            for p in range(PAIRS):
                e = jnp.exp(dot(queries[:, 128 * p : 128 * (p + 1)], Kbd[p]))
                total = dot(e.astype(BF16), ones)
                heads.append(dot((e * (1.0 / total)).astype(BF16), Vbd[p]).astype(BF16))
            out = mixed + dot(jnp.concatenate(heads, axis=1), Wo[...])
            final = silu(rms(out, g3_ref[...].reshape(1, C))).astype(BF16)
            keep = jnp.concatenate([valid[a:b] for a, b in ranges], axis=0)
            predicted = jnp.where(keep, dot(final, WF[...]), 0.0)
            x_new = scale * load(X) + beta * predicted + sigma * load(NZT, t)
            at = 0
            for a, b in ranges:
                n = b - a
                FA[a:b, :] = final[at : at + n]
                X[a:b, :] = x_new[at : at + n]
                PB[t + 1, a + COLS : b + COLS, :] = x_new[at : at + n].astype(BF16)
                at += n

        finish(((0, TOK),))

        @pl.when(t < STEPS - 1)
        def _():
            start_halo(t + 1)

        GA[...] += weight * dot(NTS[t], FA[...])
        return carry

    table = jnp.concatenate([KG[s, 80:88, :].astype(F32)[0:1] for s in range(16)], axis=0)
    ids = table[:, 0:1]
    rewards = table[:, 1:2] + table[:, 2:3] + table[:, 3:4]
    same = jnp.where(ids == prompt_ref[...].astype(F32), 1.0, 0.0)
    count = jnp.maximum(jnp.sum(same, axis=0, keepdims=True), 1.0)
    mean = jnp.sum(same * rewards, axis=0, keepdims=True) / count
    square = jnp.sum(same * (rewards * rewards), axis=0, keepdims=True) / count
    spread_1 = jnp.sqrt(jnp.maximum(square - mean * mean, 1.0))
    advantage = (reward_ref[...] - mean) / spread_1

    lax.fori_loop(0, STEPS, denoise, 0)

    lane128 = iota((FEAT, 128), 1)
    fold = spread_of(lane128 % 64, iota((FEAT, 128), 0)).astype(BF16)
    grad = sum(dot(fold, part) for part in split(GA[...])) * (advantage * (-1.0 / 16.0))
    for j in range(5):
        GS[:, j, :] = grad[:, 128 * j : 128 * (j + 1)]

    def column_copy(k):
        peer = lax.rem(dev + k, 16)
        return to_peer(GS.at[peer], GR.at[dev], r_send.at[k], r_recv.at[k], (sec, peer))

    for k in range(1, 16):
        column_copy(k).start()
    GR[dev] = GS[dev]
    flat = X[0:COLS, 0:64]
    for r in range(1, ROWS):
        flat = flat + X[r * COLS : (r + 1) * COLS, 0:64]
    flat = jnp.concatenate([flat[:, 0:32], flat[:, 32:64]], axis=0)
    x_out[...] = sum(
        lax.dot_general(part, pick, (((0,), (0,)), ((), ())), preferred_element_type=F32) for part in split(flat)
    )
    for k in range(1, 16):
        column_copy(k).wait()
    R1[...] = jnp.sum(GR[...], axis=0)

    def row_copy(k):
        return to_peer(R1, RR.at[sec], s_send.at[k], s_recv.at[k], (lax.rem(sec + k, 16), dev))

    for k in range(1, 16):
        row_copy(k).start()
    RR[sec] = R1[...]
    for k in range(1, 16):
        row_copy(k).wait()
    total = jnp.sum(RR[...], axis=0)
    picked = jnp.zeros((128, 128), F32)
    want = iota((128, 128), 0) + sec * SHARD
    for j in range(5):
        hit = iota((128, 128), 1) + 128 * j == want
        picked = jnp.where(hit, jnp.broadcast_to(total[j : j + 1], (128, 128)), picked)
    g_out[...] = jnp.sum(jnp.transpose(picked), axis=0, keepdims=True)[:, 0:SHARD]


def per_device(
    latents,
    noise,
    rewards,
    prompt_ids,
    context,
    time_bias,
    gain_first,
    gain_second,
    gain_third,
    w_in,
    w_conv,
    w_query,
    w_key,
    w_value,
    w_attn_out,
    w_final,
    moment_first,
    moment_second,
):
    words, width = context.shape[1:]
    flat_context = context.transpose(1, 0, 2).reshape(words * context.shape[0], width)
    vmem = pl.BlockSpec(memory_space=pltpu.VMEM)
    dma = pltpu.SemaphoreType.DMA
    x_new, grad = pl.pallas_call(
        body,
        out_shape=(jax.ShapeDtypeStruct((32, 128), F32), jax.ShapeDtypeStruct((1, SHARD), F32)),
        in_specs=[vmem] * 4 + [pl.BlockSpec(memory_space=pl.ANY)] + [vmem] * 11,
        out_specs=(vmem,) * 2,
        scratch_shapes=[
            pltpu.VMEM(flat_context.shape, BF16),
            pltpu.VMEM((NZ, 2, NX, 2, 2, SHARD, LANES), BF16),
            pltpu.VMEM((16, 88, 128), BF16),
            pltpu.VMEM((16, 80, 128), BF16),
            pltpu.VMEM((9 * C, C), BF16),
            pltpu.VMEM((C, C), BF16),
            pltpu.VMEM((C, C), BF16),
            pltpu.VMEM((128, C), F32),
            pltpu.VMEM((NZ, 2, SHARD, 128), F32),
            pltpu.VMEM((C, 128), BF16),
            pltpu.VMEM((128, C), BF16),
            pltpu.VMEM((PAIRS, 128, 256), BF16),
            pltpu.VMEM((PAIRS, 256, 128), BF16),
            pltpu.VMEM((STEPS + 1, TOK + 2 * COLS, 128), BF16),
            pltpu.VMEM((TOK + 2 * COLS, 3 * C), BF16),
            pltpu.VMEM((TOK, C), F32),
            pltpu.VMEM((TOK, C), F32),
            pltpu.VMEM((TOK, 128), F32),
            pltpu.VMEM((STEPS, TOK, 128), F32),
            pltpu.VMEM((STEPS, 128, TOK), BF16),
            pltpu.VMEM((TOK, C), BF16),
            pltpu.VMEM((128, C), F32),
            pltpu.VMEM((16, 8, 128), F32),
            pltpu.VMEM((16, 8, 128), F32),
            pltpu.VMEM((8, 128), F32),
            pltpu.VMEM((16, 8, 128), F32),
            dma((3, 8)),
            dma((3, 8)),
            dma((3, 4)),
            dma((3, 4)),
            dma((3, 4, 2, 4)),
            dma((3, 4, 2, 4)),
            dma((28,)),
            dma((28,)),
            dma((16,)),
            dma((16,)),
            dma((16,)),
            dma((16,)),
            dma((STEPS, 2)),
            dma((STEPS, 2)),
            dma((16,)),
            dma((16,)),
            dma((16,)),
            dma((16,)),
            dma,
        ],
        compiler_params=pltpu.CompilerParams(
            collective_id=0, has_side_effects=True, vmem_limit_bytes=58 * 1024 * 1024
        ),
        name="ddpo",
    )(
        latents.reshape(32, 128),
        noise.reshape(STEPS * 32, 128),
        rewards.reshape(1, 1),
        prompt_ids.reshape(1, 1),
        flat_context,
        time_bias,
        gain_first,
        gain_second,
        gain_third,
        w_in,
        w_conv.T,
        w_query,
        w_key.T,
        w_value.T,
        w_attn_out,
        w_final.T,
    )
    g = grad.T
    moment_one = 0.9 * moment_first + 0.1 * g
    moment_two = 0.999 * moment_second + 0.001 * g * g
    new_weight = w_final - learn_rate * moment_one / (jnp.sqrt(moment_two) + 1e-08)
    return (x_new.reshape(latents.shape), new_weight, moment_one, moment_two)


def solution(mesh):
    placed = (
        P("sec", None, "dev", None),
        P(None, "sec", None, "dev", None),
        P("sec"),
        P("sec"),
        P(),
        P(),
        P(),
        P(),
        P(),
        P("sec", "dev"),
        P("sec", "dev"),
        P("sec", "dev"),
        P("sec", "dev"),
        P("sec", "dev"),
        P("sec", "dev"),
        P("sec", "dev"),
        P("sec", "dev"),
        P("sec", "dev"),
    )
    return jax.shard_map(
        per_device,
        mesh=mesh,
        in_specs=placed,
        out_specs=(P("sec", None, "dev", None), P("sec", "dev"), P("sec", "dev"), P("sec", "dev")),
        check_vma=False,
    )
```

```python
import math

import jax
import jax.numpy as jnp
from jax import lax
from jax.experimental import pallas as pl
from jax.experimental.pallas import tpu as pltpu
from jax.sharding import PartitionSpec as P

HEAD = 64
STEPS = 6
ROWS = 4
COLS = 64
TOK = ROWS * COLS
C = 640
FEAT = 16
PAIRS = C // (2 * HEAD)
SHARD = 40
CONV_ROWS = 360
LANES = 512
FINAL_AT = 384
QUERY_AT = 400
OUT_AT = 440
IN_AT = 480
CTX_TOK = 77

alpha_bars = (0.1, 0.15, 0.21, 0.28, 0.36, 0.45, 0.55)
norm_eps = 1e-06
learn_rate = 0.001
NX, NY, NZ = 4, 4, 8
SIZE = {"x": NX, "y": NY, "z": NZ}
CLASSES = (
    ((0, 16), "zyx"),
    ((16, 32), "zxy"),
    ((32, 40), "xyz"),
)
MESH_ID = pl.DeviceIdType.MESH
F32 = jnp.float32
BF16 = jnp.bfloat16


def plan(step_index):
    current = alpha_bars[step_index]
    following = alpha_bars[step_index + 1]
    sigma = math.sqrt((1.0 - following) / (1.0 - current)) * math.sqrt(1.0 - current / following)
    scale = math.sqrt(following / current)
    beta = math.sqrt(1.0 - following - sigma * sigma) - scale * math.sqrt(1.0 - current)
    return (scale, beta, sigma)


PLANS = [plan(i) for i in range(STEPS)]


def dot(a, b):
    return jnp.dot(a, b, preferred_element_type=F32)


def dot_t(a, b):
    return lax.dot_general(a, b, (((1,), (1,)), ((), ())), preferred_element_type=F32)


def rms(values, gain):
    mean_square = jnp.mean(values * values, axis=-1, keepdims=True)
    return values * lax.rsqrt(mean_square + norm_eps) * gain


def silu(v):
    half = 0.5 * v
    return half + half * jnp.tanh(half)


def choose(index, values):
    out = jnp.float32(values[0])
    for i in range(1, len(values)):
        out = jnp.where(index == i, jnp.float32(values[i]), out)
    return out


def iota(shape, dim):
    return lax.broadcasted_iota(jnp.int32, shape, dim)


def body(
    lat_ref,
    noise_ref,
    reward_ref,
    prompt_ref,
    ctx_ref,
    bias_ref,
    g1_ref,
    g2_ref,
    g3_ref,
    w_in_ref,
    w_conv_ref,
    w_query_ref,
    w_key_ref,
    w_value_ref,
    w_out_ref,
    w_final_ref,
    x_out,
    g_out,
    CX,
    IN,
    XO,
    KO,
    G,
    KG,
    KT,
    Wc,
    Wq,
    Wo,
    Win,
    WS,
    WF,
    WI,
    Kbd,
    Vbd,
    PB,
    A,
    H,
    M,
    X,
    NZT,
    NTS,
    FA,
    GA,
    GS,
    GR,
    R1,
    RR,
    a_send,
    a_recv,
    l_send,
    l_recv,
    g_send,
    g_recv,
    b_send,
    b_recv,
    k_send,
    k_recv,
    t_send,
    t_recv,
    h_send,
    h_recv,
    r_send,
    r_recv,
    s_send,
    s_recv,
    i_send,
    i_recv,
    c_sem,
):
    sec = lax.axis_index("sec")
    dev = lax.axis_index("dev")
    z, ylo = sec // 2, sec % 2
    xx, yhi, core = dev // 4, (dev // 2) % 2, dev % 2
    yy = yhi * 2 + ylo
    me = {"x": xx, "y": yy, "z": z}

    def device(x, y, zc, c):
        return (zc * 2 + y % 2, x * 4 + (y // 2) * 2 + c)

    def neighbour(axis, delta):
        pos = dict(me)
        pos[axis] = lax.rem(me[axis] + delta + SIZE[axis], SIZE[axis])
        return device(pos["x"], pos["y"], pos["z"], core)

    image = 2 * z + yhi
    pos = 2 * (xx + ylo * (7 - 2 * xx)) + core
    column = 4 * xx + 2 * ylo + core

    def worker(i, p):
        place_q = p // 2
        side = place_q // 4
        return device(place_q + side * (7 - 2 * place_q), (i % 2) * 2 + side, i // 2, p % 2)

    stays = jnp.logical_and(image == sec, pos == dev)

    barrier = pltpu.get_barrier_semaphore()

    def greet(peer):
        pl.semaphore_signal(barrier, inc=1, device_id=peer, device_id_type=MESH_ID)

    for i in range(1, NY * NZ):
        greet(device(xx, lax.rem(yy + i // NZ, NY), lax.rem(z + i % NZ, NZ), core))
    for i in range(1, 2 * NX * NY):
        greet(device(lax.rem(xx + i // 8, NX), lax.rem(yy + (i // 2) % 4, NY), z, lax.rem(core + i % 2, 2)))

    context_copy = pltpu.make_async_copy(ctx_ref, CX, c_sem)
    context_copy.start()

    eye = (iota((SHARD, SHARD), 0) == iota((SHARD, SHARD), 1)).astype(BF16)
    lane40 = iota((SHARD, 128), 1)
    row40 = iota((SHARD, 128), 0)

    def place(square, at):
        turned = dot_t(eye, square).astype(BF16)
        return dot(turned, (lane40 == row40 + (at - FINAL_AT)).astype(BF16))

    def stand(row):
        wide = jnp.broadcast_to(row.astype(F32), (SHARD, SHARD))
        on_diagonal = iota((SHARD, SHARD), 0) == iota((SHARD, SHARD), 1)
        return jnp.sum(jnp.where(on_diagonal, wide, 0.0), axis=1, keepdims=True)

    tail = place(w_query_ref[...], QUERY_AT) + place(w_out_ref[...], OUT_AT)
    tail = jnp.where(lane40 == IN_AT - FINAL_AT, stand(w_in_ref[...]), tail)
    tail = jnp.where(lane40 == dev, stand(w_final_ref[...]), tail)
    G[z, ylo, xx, yhi, core, :, 256:FINAL_AT] = jnp.zeros((SHARD, 128), BF16)
    G[z, ylo, xx, yhi, core, :, 0:CONV_ROWS] = w_conv_ref[...]
    G[z, ylo, xx, yhi, core, :, FINAL_AT:LANES] = tail.astype(BF16)

    pick = iota((128, 128), 1) == 2 * (iota((128, 128), 0) % COLS) + iota((128, 128), 0) // COLS
    pick = pick.astype(BF16)

    def split(v):
        top = v.astype(BF16)
        rest = v - top.astype(F32)
        mid = rest.astype(BF16)
        return top, mid, (rest - mid.astype(F32)).astype(BF16)

    own_row = iota((TOK, 2 * 32), 0) // COLS == (iota((TOK, 2 * 32), 1) % 8) // 2

    def turn(rows32):
        cols = sum(dot_t(pick, part) for part in split(rows32))
        both = jnp.concatenate([cols[0:COLS], cols[COLS : 2 * COLS]], axis=1)
        return jnp.where(own_row, jnp.concatenate([both] * ROWS, axis=0), 0.0)

    pl.semaphore_wait(barrier, NY * NZ - 1 + 2 * NX * NY - 1)

    def halo_copy(t, up):
        if up:
            src, dst, to, i = PB.at[t, pl.ds(COLS, COLS)], PB.at[t, pl.ds(COLS + TOK, COLS)], pos + 15, 0
        else:
            src, dst, to, i = PB.at[t, pl.ds(TOK, COLS)], PB.at[t, pl.ds(0, COLS)], pos + 1, 1
        return pltpu.make_async_remote_copy(
            src, dst, h_send.at[t, i], h_recv.at[t, i], device_id=worker(image, lax.rem(to, 16)), device_id_type=MESH_ID
        )

    def start_halo(t):
        halo_copy(t, True).start()
        halo_copy(t, False).start()

    def wait_halo(t):
        halo_copy(t, True).wait()
        halo_copy(t, False).wait()

    def to_peer(src, dst, send, recv, peer):
        return pltpu.make_async_remote_copy(src, dst, send, recv, device_id=peer, device_id_type=MESH_ID)

    def latents_in():
        return to_peer(lat_ref, IN.at[pl.ds(0, 32)], i_send.at[0], i_recv.at[0], worker(sec, dev))

    def noise_in():
        return to_peer(noise_ref, IN.at[pl.ds(32, 32 * STEPS)], i_send.at[1], i_recv.at[1], worker(sec, dev))

    def latents_out():
        return to_peer(XO.at[0], XO.at[1], i_send.at[2], i_recv.at[2], (image, pos))

    @pl.when(jnp.logical_not(stays))
    def _():
        latents_in().start()

    def key_copy(k):
        peer = device(xx, lax.rem(yhi + k % 2, 2) * 2 + yhi, lax.rem(z + k // 2, NZ), core)
        return to_peer(KO, KG.at[sec], k_send.at[k], k_recv.at[2 * (k // 2) + ylo], peer)

    def key_arrival(i):
        return to_peer(KO, KG.at[sec], k_send.at[0], k_recv.at[i], (sec, lax.rem(dev + 1, 16)))

    sent = []
    pushes = []

    def region(rows, half, **where):
        zi, xi = where["z"], where["x"]
        zi = pl.ds(0, NZ) if zi is None else zi
        xi = pl.ds(0, NX) if xi is None else xi
        if where["y"] is None:
            lo_i, hi_i = pl.ds(0, 2), pl.ds(0, 2)
        else:
            lo_i, hi_i = where["y"] % 2, where["y"] // 2
        lanes = pl.ds(0, LANES) if half is None else pl.ds(half * (LANES // 2), LANES // 2)
        return G.at[zi, lo_i, xi, hi_i, core, pl.ds(rows[0], rows[1] - rows[0]), lanes]

    def along(axis, delta):
        return lax.rem(me[axis] + delta + SIZE[axis], SIZE[axis])

    def gather(k, rows, order):
        first, second, third = order
        n = SIZE[third]

        def block_copy(j):
            ref = region(rows, None, **me)
            return to_peer(ref, ref, a_send.at[k, j], a_recv.at[k, j], neighbour(first, j))

        def line_copy(j):
            ref = region(rows, None, **{first: None, second: me[second], third: me[third]})
            return to_peer(ref, ref, l_send.at[k, j], l_recv.at[k, j], neighbour(second, j))

        def ring_copy(j, direction, r):
            step = 1 if direction == 0 else -1
            half = direction if r == n // 2 else None
            place_ = {first: None, second: along(second, -j), third: along(third, -step * (r - 1))}
            ref = region(rows, half, **place_)
            return to_peer(
                ref, ref, g_send.at[k, j, direction, r - 1], g_recv.at[k, j, direction, r - 1], neighbour(third, step)
            )

        def push(j, delta):
            place_ = {first: None, second: None if j is None else along(second, -j), third: along(third, delta)}
            ref = region(rows, None, **place_)
            i = len(pushes)
            c = to_peer(ref, ref, b_send.at[i], b_recv.at[i], (sec, dev + 1 - 2 * core))
            c.start()
            pushes.append(c)

        def start(c):
            c.start()
            sent.append(c)

        for j in range(1, SIZE[first]):
            start(block_copy(j))
        yield
        for j in range(1, SIZE[first]):
            block_copy(j).wait_recv()
        for j in (1, 3, 2):
            start(line_copy(j))
        for direction in (0, 1):
            start(ring_copy(0, direction, 1))
        yield
        for j in (1, 3, 2):
            line_copy(j).wait_recv()
            for direction in (0, 1):
                start(ring_copy(j, direction, 1))
            yield
        push(None, 0)
        for r in range(2, n // 2 + 1):
            for j in (0, 1, 3, 2):
                for direction in (0, 1):
                    ring_copy(j, direction, r - 1).wait_recv()
                    start(ring_copy(j, direction, r))
                yield
            push(None, r - 1)
            push(None, -(r - 1))
        for j in (0, 1, 3, 2):
            for direction in (0, 1):
                ring_copy(j, direction, n // 2).wait_recv()
            push(j, n // 2)
            yield

    def keys_and_values():
        KO[0:SHARD, :] = w_key_ref[...]
        KO[SHARD : 2 * SHARD, :] = w_value_ref[...]
        reward = jnp.broadcast_to(reward_ref[...], (8, 128))
        prompt = jnp.broadcast_to(prompt_ref[...].astype(F32), (8, 128))
        hi = reward.astype(BF16).astype(F32)
        mid = (reward - hi).astype(BF16).astype(F32)
        low = reward - hi - mid
        lane8 = iota((8, 128), 1)
        stats = jnp.where(lane8 == 0, prompt, 0.0)
        for i, part in enumerate((hi, mid, low)):
            stats = jnp.where(lane8 == i + 1, part, stats)
        KO[80:88, :] = stats.astype(BF16)
        for k in range(1, 16):
            key_copy(k).start()

        @pl.when(ylo != yhi)
        def _():
            key_copy(0).start()

        @pl.when(ylo == yhi)
        def _():
            KG[sec] = KO[...]

        yield
        yield
        yield
        yield
        yield
        yield
        yield
        yield
        for k in range(1, 16):
            key_copy(k).wait_send()

        @pl.when(ylo != yhi)
        def _():
            key_copy(0).wait_send()

        for i in range(2, 16):
            key_arrival(i).wait_recv()
        key_arrival(1 - ylo).wait_recv()

        @pl.when(ylo != yhi)
        def _():
            key_arrival(ylo).wait_recv()

        wide = jnp.concatenate([KG[s, 0:80, :] for s in range(16)], axis=1)
        context_copy.wait()
        every = dot_t(wide, CX[...]).astype(BF16)
        n = CX.shape[0]
        own_prompt = KG[image, 80:88, :].astype(F32)[0:1, 0:1]
        mine = (iota((n, 128), 0) - 8 * iota((n, 128), 1)).astype(F32) == own_prompt
        KT[column] = dot(every, mine.astype(BF16)).astype(BF16)

        def copy(k):
            peer = worker(image, lax.rem(pos + k, 16))
            return to_peer(KT.at[column], KT.at[column], t_send.at[k], t_recv.at[k], peer)

        for k in range(1, 16):
            copy(k).start()
        yield
        yield
        yield
        yield
        yield
        yield
        for k in range(1, 16):
            copy(k).wait()
        kt = jnp.concatenate([KT[d, 0:SHARD, :] for d in range(16)], axis=0)
        vt = jnp.concatenate([KT[d, SHARD : 2 * SHARD, :] for d in range(16)], axis=0)
        v = jnp.transpose(vt.astype(F32))
        row = iota((128, 128), 0)
        lane = iota((128, 128), 1)
        for p in range(PAIRS):
            part = kt[128 * p : 128 * (p + 1), :].astype(F32) * (1.0 / math.sqrt(HEAD))
            Kbd[p, :, 0:128] = jnp.where(row < HEAD, part, 0.0).astype(BF16)
            Kbd[p, :, 128:256] = jnp.where(row < HEAD, 0.0, part).astype(BF16)
            part = v[:, 128 * p : 128 * (p + 1)]
            Vbd[p, 0:128, :] = jnp.where(lane < HEAD, part, 0.0).astype(BF16)
            Vbd[p, 128:256, :] = jnp.where(lane < HEAD, 0.0, part).astype(BF16)

    def tokens():
        @pl.when(jnp.logical_not(stays))
        def _():
            noise_in().start()
            latents_in().wait()

        @pl.when(stays)
        def _():
            IN[0:32, :] = lat_ref[...]
            IN[32:, :] = noise_ref[...]

        X[...] = jnp.zeros_like(X)
        X[:, 0:64] = turn(IN[0:32, :])
        PB[0, COLS : COLS + TOK, :] = X[...].astype(BF16)
        start_halo(0)
        yield
        yield
        @pl.when(jnp.logical_not(stays))
        def _():
            noise_in().wait()

        GA[...] = jnp.zeros_like(GA)
        GS[...] = jnp.zeros_like(GS)
        Win[...] = jnp.zeros_like(Win)
        for t in range(STEPS):
            yield
            yield
            nt = turn(IN[32 * (t + 1) : 32 * (t + 2), :])
            NZT[t] = jnp.concatenate([nt, jnp.zeros_like(nt)], axis=1)
            top = nt.astype(BF16).astype(F32)
            NTS[t] = jnp.transpose(jnp.concatenate([top, nt - top], axis=1)).astype(BF16)

    running = [gather(k, rows, order) for k, (rows, order) in enumerate(CLASSES)]
    running += [keys_and_values(), tokens()]
    while running:
        left = []
        for g in running:
            try:
                next(g)
                left.append(g)
            except StopIteration:
                pass
        running = left
    for c in sent:
        c.wait_send()
    for c in pushes:
        c.wait()

    lane_w = iota((SHARD, 128), 1)

    def settle(zi, carry):
        turned = []
        for lo in range(2):
            parts = G[zi, lo].astype(F32)
            flat = parts.reshape(C, LANES)
            tail = jnp.sum(parts.reshape(16, SHARD, LANES)[:, :, FINAL_AT:LANES], axis=0)
            WS[zi, lo] = jnp.where(lane_w < FEAT, tail, 0.0)
            turned.append(jnp.transpose(flat))
        conv = jnp.concatenate([w[0:CONV_ROWS] for w in turned], axis=0).astype(BF16)
        Wc[pl.ds(pl.multiple_of(zi * 2 * CONV_ROWS, 16), 2 * CONV_ROWS), :] = conv
        at = pl.ds(pl.multiple_of(zi * 2 * SHARD, 16), 2 * SHARD)
        Wq[at, :] = jnp.concatenate([w[QUERY_AT : QUERY_AT + SHARD] for w in turned], axis=0).astype(BF16)
        Wo[at, :] = jnp.concatenate([w[OUT_AT : OUT_AT + SHARD] for w in turned], axis=0).astype(BF16)
        for lo in range(2):
            Win[pl.ds(zi * 2 + lo, 1), :] = turned[lo][IN_AT : IN_AT + 1]
        return carry

    lax.fori_loop(0, NZ, settle, 0)

    def spread_of(lane, feature):
        return (lane < 64) & (feature == ((lane // 8) % 4) * 4 + (lane % 2) * 2 + lane // 32)

    by_col = spread_of(iota((128, 128), 1), iota((128, 128), 0)).astype(BF16)
    by_row = spread_of(iota((128, 128), 0), iota((128, 128), 1)).astype(BF16)
    WF[...] = dot(WS[...].reshape(C, 128).astype(BF16), by_col).astype(BF16)
    WI[...] = dot(by_row, Win[...].astype(BF16)).astype(BF16)
    valid = iota((TOK, 128), 0) // COLS == (iota((TOK, 128), 1) % 8) // 2

    real = iota((1, 128), 1) < CTX_TOK

    def spread(act, at, n):
        col = iota((n, C), 0) % COLS
        rows = pl.ds(at, n)
        A[rows, C : 2 * C] = act.astype(BF16)
        A[rows, 0:C] = jnp.where(col == 0, 0.0, pltpu.roll(act, 1, 0)).astype(BF16)
        A[rows, 2 * C : 3 * C] = jnp.where(col == COLS - 1, 0.0, pltpu.roll(act, n - 1, 0)).astype(BF16)

    def denoise(t, carry):
        scale = choose(t, [p[0] for p in PLANS])
        beta = choose(t, [p[1] for p in PLANS])
        sigma = choose(t, [p[2] for p in PLANS])
        weight = choose(t, [p[1] / p[2] for p in PLANS])
        bias = bias_ref[pl.ds(t, 1), :]
        w_first = WI[...]
        hidden = dot(PB[t, COLS : COLS + TOK, :], w_first) + bias
        H[...] = hidden
        spread(silu(rms(hidden, g1_ref[...].reshape(1, C))), COLS, TOK)
        inner = TOK - COLS
        M[...] = H[...] + dot(A[COLS : COLS + TOK, :], Wc[3 * C : 6 * C, :])
        M[COLS:TOK, :] += dot(A[COLS:TOK, :], Wc[0 : 3 * C, :])
        wait_halo(t)
        M[0:inner, :] += dot(A[2 * COLS : COLS + TOK, :], Wc[6 * C : 9 * C, :])
        edge = jnp.concatenate([PB[t, 0:COLS, :], PB[t, COLS + TOK :, :]], axis=0)
        act = silu(rms(dot(edge, w_first) + bias, g1_ref[...].reshape(1, C)))
        above = jnp.where(pos > 0, act[0:COLS], 0.0)
        below = jnp.where(pos < 15, act[COLS:], 0.0)
        spread(above, 0, COLS)
        spread(below, COLS + TOK, COLS)
        M[0:COLS, :] += dot(A[0:COLS, :], Wc[0 : 3 * C, :])
        M[inner:TOK, :] += dot(A[COLS + TOK :, :], Wc[6 * C : 9 * C, :])

        mixed = M[...]
        normed = rms(mixed, g2_ref[...].reshape(1, C)).astype(BF16)
        queries = dot(normed, Wq[...]).astype(BF16)
        heads = []
        for p in range(PAIRS):
            e = jnp.exp(dot(queries[:, 128 * p : 128 * (p + 1)], Kbd[p]))
            shares = []
            for half in (e[:, 0:128], e[:, 128:256]):
                total = jnp.sum(jnp.where(real, half, 0.0), axis=1, keepdims=True)
                shares.append(half * (1.0 / total))
            heads.append(dot(jnp.concatenate(shares, axis=1).astype(BF16), Vbd[p]).astype(BF16))
        out = mixed + dot(jnp.concatenate(heads, axis=1), Wo[...])

        def finish(ranges):
            def part(v):
                return jnp.concatenate([v[a:b] for a, b in ranges], axis=0)

            def load(ref, *lead):
                return jnp.concatenate([ref[(*lead, slice(a, b))] for a, b in ranges], axis=0)

            final = silu(rms(part(out), g3_ref[...].reshape(1, C))).astype(BF16)
            predicted = jnp.where(part(valid), dot(final, WF[...]), 0.0)
            x_new = scale * load(X) + beta * predicted + sigma * load(NZT, t)
            at = 0
            for a, b in ranges:
                n = b - a
                FA[a:b, :] = final[at : at + n]
                X[a:b, :] = x_new[at : at + n]
                PB[t + 1, a + COLS : b + COLS, :] = x_new[at : at + n].astype(BF16)
                at += n

        finish(((0, COLS), (TOK - COLS, TOK)))

        @pl.when(t < STEPS - 1)
        def _():
            start_halo(t + 1)

        finish(((COLS, TOK - COLS),))
        GA[...] += weight * dot(NTS[t], FA[...])
        return carry

    table = jnp.concatenate([KG[s, 80:88, :].astype(F32)[0:1] for s in range(16)], axis=0)
    ids = table[:, 0:1]
    rewards = table[:, 1:2] + table[:, 2:3] + table[:, 3:4]
    here = iota((16, 1), 0) == image
    own_id = jnp.sum(jnp.where(here, ids, 0.0), axis=0, keepdims=True)
    own_reward = jnp.sum(jnp.where(here, rewards, 0.0), axis=0, keepdims=True)
    same = jnp.where(ids == own_id, 1.0, 0.0)
    count = jnp.maximum(jnp.sum(same, axis=0, keepdims=True), 1.0)
    mean = jnp.sum(same * rewards, axis=0, keepdims=True) / count
    square = jnp.sum(same * (rewards * rewards), axis=0, keepdims=True) / count
    spread_1 = jnp.sqrt(jnp.maximum(square - mean * mean, 1.0))
    advantage = (own_reward - mean) / spread_1

    lax.fori_loop(0, STEPS, denoise, 0)

    lane128 = iota((FEAT, 128), 1)
    fold = spread_of(lane128 % 64, iota((FEAT, 128), 0)).astype(BF16)
    grad = sum(dot(fold, part) for part in split(GA[...])) * (advantage * (-1.0 / 16.0))
    for j in range(5):
        GS[:, j, :] = grad[:, 128 * j : 128 * (j + 1)]

    def column_copy(k):
        peer = lax.rem(dev + k, 16)
        return to_peer(GS.at[peer], GR.at[dev], r_send.at[k], r_recv.at[k], (sec, peer))

    for k in range(1, 16):
        column_copy(k).start()
    GR[dev] = GS[dev]
    flat = X[0:COLS, 0:64]
    for r in range(1, ROWS):
        flat = flat + X[r * COLS : (r + 1) * COLS, 0:64]
    flat = jnp.concatenate([flat[:, 0:32], flat[:, 32:64]], axis=0)
    XO[0] = sum(
        lax.dot_general(part, pick, (((0,), (0,)), ((), ())), preferred_element_type=F32) for part in split(flat)
    )

    @pl.when(jnp.logical_not(stays))
    def _():
        latents_out().start()

    for k in range(1, 16):
        column_copy(k).wait()
    R1[...] = jnp.sum(GR[...], axis=0)

    def row_copy(k):
        return to_peer(R1, RR.at[sec], s_send.at[k], s_recv.at[k], (lax.rem(sec + k, 16), dev))

    for k in range(1, 16):
        row_copy(k).start()
    RR[sec] = R1[...]
    for k in range(1, 16):
        row_copy(k).wait()
    total = jnp.sum(RR[...], axis=0)
    picked = jnp.zeros((128, 128), F32)
    want = iota((128, 128), 0) + sec * SHARD
    for j in range(5):
        hit = iota((128, 128), 1) + 128 * j == want
        picked = jnp.where(hit, jnp.broadcast_to(total[j : j + 1], (128, 128)), picked)
    @pl.when(jnp.logical_not(stays))
    def _():
        latents_out().wait()
        x_out[...] = XO[1]

    @pl.when(stays)
    def _():
        x_out[...] = XO[0]

    g_out[...] = jnp.sum(jnp.transpose(picked), axis=0, keepdims=True)[:, 0:SHARD]


def per_device(
    latents,
    noise,
    rewards,
    prompt_ids,
    context,
    time_bias,
    gain_first,
    gain_second,
    gain_third,
    w_in,
    w_conv,
    w_query,
    w_key,
    w_value,
    w_attn_out,
    w_final,
    moment_first,
    moment_second,
):
    words, width = context.shape[1:]
    flat_context = context.transpose(1, 0, 2).reshape(words * context.shape[0], width)
    vmem = pl.BlockSpec(memory_space=pltpu.VMEM)
    dma = pltpu.SemaphoreType.DMA
    x_new, grad = pl.pallas_call(
        body,
        out_shape=(jax.ShapeDtypeStruct((32, 128), F32), jax.ShapeDtypeStruct((1, SHARD), F32)),
        in_specs=[vmem] * 4 + [pl.BlockSpec(memory_space=pl.ANY)] + [vmem] * 11,
        out_specs=(vmem,) * 2,
        scratch_shapes=[
            pltpu.VMEM(flat_context.shape, BF16),
            pltpu.VMEM((32 * (STEPS + 1), 128), F32),
            pltpu.VMEM((2, 32, 128), F32),
            pltpu.VMEM((88, 128), BF16),
            pltpu.VMEM((NZ, 2, NX, 2, 2, SHARD, LANES), BF16),
            pltpu.VMEM((16, 88, 128), BF16),
            pltpu.VMEM((16, 80, 128), BF16),
            pltpu.VMEM((9 * C, C), BF16),
            pltpu.VMEM((C, C), BF16),
            pltpu.VMEM((C, C), BF16),
            pltpu.VMEM((128, C), F32),
            pltpu.VMEM((NZ, 2, SHARD, 128), F32),
            pltpu.VMEM((C, 128), BF16),
            pltpu.VMEM((128, C), BF16),
            pltpu.VMEM((PAIRS, 128, 256), BF16),
            pltpu.VMEM((PAIRS, 256, 128), BF16),
            pltpu.VMEM((STEPS + 1, TOK + 2 * COLS, 128), BF16),
            pltpu.VMEM((TOK + 2 * COLS, 3 * C), BF16),
            pltpu.VMEM((TOK, C), F32),
            pltpu.VMEM((TOK, C), F32),
            pltpu.VMEM((TOK, 128), F32),
            pltpu.VMEM((STEPS, TOK, 128), F32),
            pltpu.VMEM((STEPS, 128, TOK), BF16),
            pltpu.VMEM((TOK, C), BF16),
            pltpu.VMEM((128, C), F32),
            pltpu.VMEM((16, 8, 128), F32),
            pltpu.VMEM((16, 8, 128), F32),
            pltpu.VMEM((8, 128), F32),
            pltpu.VMEM((16, 8, 128), F32),
            dma((3, 8)),
            dma((3, 8)),
            dma((3, 4)),
            dma((3, 4)),
            dma((3, 4, 2, 4)),
            dma((3, 4, 2, 4)),
            dma((28,)),
            dma((28,)),
            dma((16,)),
            dma((16,)),
            dma((16,)),
            dma((16,)),
            dma((STEPS, 2)),
            dma((STEPS, 2)),
            dma((16,)),
            dma((16,)),
            dma((16,)),
            dma((16,)),
            dma((3,)),
            dma((3,)),
            dma,
        ],
        compiler_params=pltpu.CompilerParams(
            collective_id=0, has_side_effects=True, vmem_limit_bytes=58 * 1024 * 1024
        ),
        name="ddpo",
    )(
        latents.reshape(32, 128),
        noise.reshape(STEPS * 32, 128),
        rewards.reshape(1, 1),
        prompt_ids.reshape(1, 1),
        flat_context,
        time_bias,
        gain_first,
        gain_second,
        gain_third,
        w_in,
        w_conv.T,
        w_query,
        w_key.T,
        w_value.T,
        w_attn_out,
        w_final.T,
    )
    g = grad.T
    moment_one = 0.9 * moment_first + 0.1 * g
    moment_two = 0.999 * moment_second + 0.001 * g * g
    new_weight = w_final - learn_rate * moment_one / (jnp.sqrt(moment_two) + 1e-08)
    return (x_new.reshape(latents.shape), new_weight, moment_one, moment_two)


def solution(mesh):
    placed = (
        P("sec", None, "dev", None),
        P(None, "sec", None, "dev", None),
        P("sec"),
        P("sec"),
        P(),
        P(),
        P(),
        P(),
        P(),
        P("sec", "dev"),
        P("sec", "dev"),
        P("sec", "dev"),
        P("sec", "dev"),
        P("sec", "dev"),
        P("sec", "dev"),
        P("sec", "dev"),
        P("sec", "dev"),
        P("sec", "dev"),
    )
    return jax.shard_map(
        per_device,
        mesh=mesh,
        in_specs=placed,
        out_specs=(P("sec", None, "dev", None), P("sec", "dev"), P("sec", "dev"), P("sec", "dev")),
        check_vma=False,
    )
```

```python
import math

import jax
import jax.numpy as jnp
from jax import lax
from jax.experimental import pallas as pl
from jax.experimental.pallas import tpu as pltpu
from jax.sharding import PartitionSpec as P

HEAD = 64
STEPS = 6
ROWS = 4
COLS = 64
TOK = ROWS * COLS
C = 640
FEAT = 16
PAIRS = C // (2 * HEAD)
SHARD = 40
CONV_ROWS = 360
LANES = 512
FINAL_AT = 384
QUERY_AT = 400
OUT_AT = 440
IN_AT = 480
CTX_TOK = 77

alpha_bars = (0.1, 0.15, 0.21, 0.28, 0.36, 0.45, 0.55)
norm_eps = 1e-06
learn_rate = 0.001
NX, NY, NZ = 4, 4, 8
SIZE = {"x": NX, "y": NY, "z": NZ}
CLASSES = (
    ((0, 16), "zyx"),
    ((16, 32), "zxy"),
    ((32, 40), "xyz"),
)
MESH_ID = pl.DeviceIdType.MESH
F32 = jnp.float32
BF16 = jnp.bfloat16


def plan(step_index):
    current = alpha_bars[step_index]
    following = alpha_bars[step_index + 1]
    sigma = math.sqrt((1.0 - following) / (1.0 - current)) * math.sqrt(1.0 - current / following)
    scale = math.sqrt(following / current)
    beta = math.sqrt(1.0 - following - sigma * sigma) - scale * math.sqrt(1.0 - current)
    return (scale, beta, sigma)


PLANS = [plan(i) for i in range(STEPS)]


def dot(a, b):
    return jnp.dot(a, b, preferred_element_type=F32)


def dot_t(a, b):
    return lax.dot_general(a, b, (((1,), (1,)), ((), ())), preferred_element_type=F32)


def rms(values, gain):
    mean_square = jnp.mean(values * values, axis=-1, keepdims=True)
    return values * lax.rsqrt(mean_square + norm_eps) * gain


def silu(v):
    half = 0.5 * v
    return half + half * jnp.tanh(half)


def choose(index, values):
    out = jnp.float32(values[0])
    for i in range(1, len(values)):
        out = jnp.where(index == i, jnp.float32(values[i]), out)
    return out


def iota(shape, dim):
    return lax.broadcasted_iota(jnp.int32, shape, dim)


def body(
    lat_ref,
    noise_ref,
    reward_ref,
    prompt_ref,
    ctx_ref,
    bias_ref,
    g1_ref,
    g2_ref,
    g3_ref,
    w_in_ref,
    w_conv_ref,
    w_query_ref,
    w_key_ref,
    w_value_ref,
    w_out_ref,
    w_final_ref,
    x_out,
    g_out,
    CX,
    IN,
    XO,
    KO,
    G,
    KG,
    KT,
    Wc,
    Wq,
    Wo,
    Win,
    WS,
    WF,
    WI,
    Kbd,
    Vbd,
    PB,
    A,
    M,
    X,
    NZT,
    NTS,
    FA,
    GA,
    GS,
    GR,
    R1,
    RR,
    a_send,
    a_recv,
    l_send,
    l_recv,
    g_send,
    g_recv,
    b_send,
    b_recv,
    k_send,
    k_recv,
    t_send,
    t_recv,
    h_send,
    h_recv,
    r_send,
    r_recv,
    s_send,
    s_recv,
    i_send,
    i_recv,
    c_sem,
):
    sec = lax.axis_index("sec")
    dev = lax.axis_index("dev")
    z, ylo = sec // 2, sec % 2
    xx, yhi, core = dev // 4, (dev // 2) % 2, dev % 2
    yy = yhi * 2 + ylo
    me = {"x": xx, "y": yy, "z": z}

    def device(x, y, zc, c):
        return (zc * 2 + y % 2, x * 4 + (y // 2) * 2 + c)

    def neighbour(axis, delta):
        pos = dict(me)
        pos[axis] = lax.rem(me[axis] + delta + SIZE[axis], SIZE[axis])
        return device(pos["x"], pos["y"], pos["z"], core)

    image = 2 * z + yhi
    pos = 2 * (xx + ylo * (7 - 2 * xx)) + core
    column = 4 * xx + 2 * ylo + core

    def worker(i, p):
        place_q = p // 2
        side = place_q // 4
        return device(place_q + side * (7 - 2 * place_q), (i % 2) * 2 + side, i // 2, p % 2)

    stays = jnp.logical_and(image == sec, pos == dev)

    barrier = pltpu.get_barrier_semaphore()

    def greet(peer):
        pl.semaphore_signal(barrier, inc=1, device_id=peer, device_id_type=MESH_ID)

    for i in range(1, NY * NZ):
        greet(device(xx, lax.rem(yy + i // NZ, NY), lax.rem(z + i % NZ, NZ), core))
    for i in range(1, 2 * NX * NY):
        greet(device(lax.rem(xx + i // 8, NX), lax.rem(yy + (i // 2) % 4, NY), z, lax.rem(core + i % 2, 2)))

    context_copy = pltpu.make_async_copy(ctx_ref, CX, c_sem)
    context_copy.start()

    eye = (iota((SHARD, SHARD), 0) == iota((SHARD, SHARD), 1)).astype(BF16)
    lane40 = iota((SHARD, 128), 1)
    row40 = iota((SHARD, 128), 0)

    def place(square, at):
        turned = dot_t(eye, square).astype(BF16)
        return dot(turned, (lane40 == row40 + (at - FINAL_AT)).astype(BF16))

    def stand(row):
        wide = jnp.broadcast_to(row.astype(F32), (SHARD, SHARD))
        on_diagonal = iota((SHARD, SHARD), 0) == iota((SHARD, SHARD), 1)
        return jnp.sum(jnp.where(on_diagonal, wide, 0.0), axis=1, keepdims=True)

    tail = place(w_query_ref[...], QUERY_AT) + place(w_out_ref[...], OUT_AT)
    tail = jnp.where(lane40 == IN_AT - FINAL_AT, stand(w_in_ref[...]), tail)
    tail = jnp.where(lane40 == dev, stand(w_final_ref[...]), tail)
    G[z, ylo, xx, yhi, core, :, 256:FINAL_AT] = jnp.zeros((SHARD, 128), BF16)
    G[z, ylo, xx, yhi, core, :, 0:CONV_ROWS] = w_conv_ref[...]
    G[z, ylo, xx, yhi, core, :, FINAL_AT:LANES] = tail.astype(BF16)

    pick = iota((128, 128), 1) == 2 * (iota((128, 128), 0) % COLS) + iota((128, 128), 0) // COLS
    pick = pick.astype(BF16)

    def split(v):
        top = v.astype(BF16)
        rest = v - top.astype(F32)
        mid = rest.astype(BF16)
        return top, mid, (rest - mid.astype(F32)).astype(BF16)

    own_row = iota((TOK, 2 * 32), 0) // COLS == (iota((TOK, 2 * 32), 1) % 8) // 2

    def turn(rows32):
        cols = sum(dot_t(pick, part) for part in split(rows32))
        both = jnp.concatenate([cols[0:COLS], cols[COLS : 2 * COLS]], axis=1)
        return jnp.where(own_row, jnp.concatenate([both] * ROWS, axis=0), 0.0)

    pl.semaphore_wait(barrier, NY * NZ - 1 + 2 * NX * NY - 1)

    def halo_copy(t, up):
        if up:
            src, dst, to, i = PB.at[t, pl.ds(COLS, COLS)], PB.at[t, pl.ds(COLS + TOK, COLS)], pos + 15, 0
        else:
            src, dst, to, i = PB.at[t, pl.ds(TOK, COLS)], PB.at[t, pl.ds(0, COLS)], pos + 1, 1
        return pltpu.make_async_remote_copy(
            src, dst, h_send.at[t, i], h_recv.at[t, i], device_id=worker(image, lax.rem(to, 16)), device_id_type=MESH_ID
        )

    def start_halo(t):
        halo_copy(t, True).start()
        halo_copy(t, False).start()

    def wait_halo(t):
        halo_copy(t, True).wait()
        halo_copy(t, False).wait()

    def to_peer(src, dst, send, recv, peer):
        return pltpu.make_async_remote_copy(src, dst, send, recv, device_id=peer, device_id_type=MESH_ID)

    def latents_in():
        return to_peer(lat_ref, IN.at[pl.ds(0, 32)], i_send.at[0], i_recv.at[0], worker(sec, dev))

    def noise_in():
        return to_peer(noise_ref, IN.at[pl.ds(32, 32 * STEPS)], i_send.at[1], i_recv.at[1], worker(sec, dev))

    def latents_out():
        return to_peer(XO.at[0], XO.at[1], i_send.at[2], i_recv.at[2], (image, pos))

    @pl.when(jnp.logical_not(stays))
    def _():
        latents_in().start()

    def key_copy(k):
        peer = device(xx, lax.rem(yhi + k % 2, 2) * 2 + yhi, lax.rem(z + k // 2, NZ), core)
        return to_peer(KO, KG.at[sec], k_send.at[k], k_recv.at[2 * (k // 2) + ylo], peer)

    def key_arrival(i):
        return to_peer(KO, KG.at[sec], k_send.at[0], k_recv.at[i], (sec, lax.rem(dev + 1, 16)))

    sent = []
    pushes = []

    def region(rows, half, **where):
        zi, xi = where["z"], where["x"]
        zi = pl.ds(0, NZ) if zi is None else zi
        xi = pl.ds(0, NX) if xi is None else xi
        if where["y"] is None:
            lo_i, hi_i = pl.ds(0, 2), pl.ds(0, 2)
        else:
            lo_i, hi_i = where["y"] % 2, where["y"] // 2
        lanes = pl.ds(0, LANES) if half is None else pl.ds(half * (LANES // 2), LANES // 2)
        return G.at[zi, lo_i, xi, hi_i, core, pl.ds(rows[0], rows[1] - rows[0]), lanes]

    def along(axis, delta):
        return lax.rem(me[axis] + delta + SIZE[axis], SIZE[axis])

    def gather(k, rows, order):
        first, second, third = order
        n = SIZE[third]

        def block_copy(j):
            ref = region(rows, None, **me)
            return to_peer(ref, ref, a_send.at[k, j], a_recv.at[k, j], neighbour(first, j))

        def line_copy(j):
            ref = region(rows, None, **{first: None, second: me[second], third: me[third]})
            return to_peer(ref, ref, l_send.at[k, j], l_recv.at[k, j], neighbour(second, j))

        def ring_copy(j, direction, r):
            step = 1 if direction == 0 else -1
            half = direction if r == n // 2 else None
            place_ = {first: None, second: along(second, -j), third: along(third, -step * (r - 1))}
            ref = region(rows, half, **place_)
            return to_peer(
                ref, ref, g_send.at[k, j, direction, r - 1], g_recv.at[k, j, direction, r - 1], neighbour(third, step)
            )

        def push(j, delta):
            place_ = {first: None, second: None if j is None else along(second, -j), third: along(third, delta)}
            ref = region(rows, None, **place_)
            i = len(pushes)
            c = to_peer(ref, ref, b_send.at[i], b_recv.at[i], (sec, dev + 1 - 2 * core))
            c.start()
            pushes.append(c)

        def start(c):
            c.start()
            sent.append(c)

        for j in range(1, SIZE[first]):
            start(block_copy(j))
        yield
        for j in range(1, SIZE[first]):
            block_copy(j).wait_recv()
        for j in (1, 3, 2):
            start(line_copy(j))
        for direction in (0, 1):
            start(ring_copy(0, direction, 1))
        yield
        for j in (1, 3, 2):
            line_copy(j).wait_recv()
            for direction in (0, 1):
                start(ring_copy(j, direction, 1))
            yield
        push(None, 0)
        for r in range(2, n // 2 + 1):
            for j in (0, 1, 3, 2):
                for direction in (0, 1):
                    ring_copy(j, direction, r - 1).wait_recv()
                    start(ring_copy(j, direction, r))
                yield
            push(None, r - 1)
            push(None, -(r - 1))
        for j in (0, 1, 3, 2):
            for direction in (0, 1):
                ring_copy(j, direction, n // 2).wait_recv()
            push(j, n // 2)
            yield

    def keys_and_values():
        KO[0:SHARD, :] = w_key_ref[...]
        KO[SHARD : 2 * SHARD, :] = w_value_ref[...]
        reward = jnp.broadcast_to(reward_ref[...], (8, 128))
        prompt = jnp.broadcast_to(prompt_ref[...].astype(F32), (8, 128))
        hi = reward.astype(BF16).astype(F32)
        mid = (reward - hi).astype(BF16).astype(F32)
        low = reward - hi - mid
        lane8 = iota((8, 128), 1)
        stats = jnp.where(lane8 == 0, prompt, 0.0)
        for i, part in enumerate((hi, mid, low)):
            stats = jnp.where(lane8 == i + 1, part, stats)
        KO[80:88, :] = stats.astype(BF16)
        for k in range(1, 16):
            key_copy(k).start()

        @pl.when(ylo != yhi)
        def _():
            key_copy(0).start()

        @pl.when(ylo == yhi)
        def _():
            KG[sec] = KO[...]

        yield
        yield
        yield
        yield
        yield
        yield
        yield
        yield
        for k in range(1, 16):
            key_copy(k).wait_send()

        @pl.when(ylo != yhi)
        def _():
            key_copy(0).wait_send()

        for i in range(2, 16):
            key_arrival(i).wait_recv()
        key_arrival(1 - ylo).wait_recv()

        @pl.when(ylo != yhi)
        def _():
            key_arrival(ylo).wait_recv()

        wide = jnp.concatenate([KG[s, 0:80, :] for s in range(16)], axis=1)
        context_copy.wait()
        every = dot_t(CX[...], wide).astype(BF16)
        n = CX.shape[0]
        own_prompt = KG[image, 80:88, :].astype(F32)[0:1, 0:1]
        mine = (iota((128, n), 1) - 8 * iota((128, n), 0)).astype(F32) == own_prompt
        own = dot(mine.astype(BF16), every)
        own = jnp.concatenate([own, jnp.zeros((128, 48), F32)], axis=1)
        KT[column] = jnp.transpose(own)[0:80].astype(BF16)

        def copy(k):
            peer = worker(image, lax.rem(pos + k, 16))
            return to_peer(KT.at[column], KT.at[column], t_send.at[k], t_recv.at[k], peer)

        for k in range(1, 16):
            copy(k).start()
        yield
        yield
        yield
        yield
        yield
        yield
        for k in range(1, 16):
            copy(k).wait()
        kt = jnp.concatenate([KT[d, 0:SHARD, :] for d in range(16)], axis=0)
        vt = jnp.concatenate([KT[d, SHARD : 2 * SHARD, :] for d in range(16)], axis=0)
        v = jnp.transpose(vt.astype(F32))
        row = iota((128, 128), 0)
        lane = iota((128, 128), 1)
        for p in range(PAIRS):
            part = kt[128 * p : 128 * (p + 1), :].astype(F32) * (1.0 / math.sqrt(HEAD))
            Kbd[p, :, 0:128] = jnp.where(row < HEAD, part, 0.0).astype(BF16)
            Kbd[p, :, 128:256] = jnp.where(row < HEAD, 0.0, part).astype(BF16)
            part = v[:, 128 * p : 128 * (p + 1)]
            Vbd[p, 0:128, :] = jnp.where(lane < HEAD, part, 0.0).astype(BF16)
            Vbd[p, 128:256, :] = jnp.where(lane < HEAD, 0.0, part).astype(BF16)

    def tokens():
        @pl.when(jnp.logical_not(stays))
        def _():
            noise_in().start()
            latents_in().wait()

        @pl.when(stays)
        def _():
            IN[0:32, :] = lat_ref[...]
            IN[32:, :] = noise_ref[...]

        X[...] = jnp.zeros_like(X)
        X[:, 0:64] = turn(IN[0:32, :])
        PB[0, COLS : COLS + TOK, :] = X[...].astype(BF16)
        start_halo(0)
        yield
        yield
        @pl.when(jnp.logical_not(stays))
        def _():
            noise_in().wait()

        GA[...] = jnp.zeros_like(GA)
        GS[...] = jnp.zeros_like(GS)
        Win[...] = jnp.zeros_like(Win)
        for t in range(STEPS):
            yield
            yield
            nt = turn(IN[32 * (t + 1) : 32 * (t + 2), :])
            NZT[t] = jnp.concatenate([nt, jnp.zeros_like(nt)], axis=1)
            top = nt.astype(BF16).astype(F32)
            NTS[t] = jnp.transpose(jnp.concatenate([top, nt - top], axis=1)).astype(BF16)

    running = [gather(k, rows, order) for k, (rows, order) in enumerate(CLASSES)]
    running += [keys_and_values(), tokens()]
    while running:
        left = []
        for g in running:
            try:
                next(g)
                left.append(g)
            except StopIteration:
                pass
        running = left
    for c in sent:
        c.wait_send()
    for c in pushes:
        c.wait()

    lane_w = iota((SHARD, 128), 1)

    def settle(zi, carry):
        turned = []
        for lo in range(2):
            parts = G[zi, lo].astype(F32)
            flat = parts.reshape(C, LANES)
            tail = jnp.sum(parts.reshape(16, SHARD, LANES)[:, :, FINAL_AT:LANES], axis=0)
            WS[zi, lo] = jnp.where(lane_w < FEAT, tail, 0.0)
            turned.append(jnp.transpose(flat))
        conv = jnp.concatenate([w[0:CONV_ROWS] for w in turned], axis=0).astype(BF16)
        Wc[pl.ds(pl.multiple_of(zi * 2 * CONV_ROWS, 16), 2 * CONV_ROWS), :] = conv
        at = pl.ds(pl.multiple_of(zi * 2 * SHARD, 16), 2 * SHARD)
        Wq[at, :] = jnp.concatenate([w[QUERY_AT : QUERY_AT + SHARD] for w in turned], axis=0).astype(BF16)
        Wo[at, :] = jnp.concatenate([w[OUT_AT : OUT_AT + SHARD] for w in turned], axis=0).astype(BF16)
        for lo in range(2):
            Win[pl.ds(zi * 2 + lo, 1), :] = turned[lo][IN_AT : IN_AT + 1]
        return carry

    lax.fori_loop(0, NZ, settle, 0)

    def spread_of(lane, feature):
        return (lane < 64) & (feature == ((lane // 8) % 4) * 4 + (lane % 2) * 2 + lane // 32)

    by_col = spread_of(iota((128, 128), 1), iota((128, 128), 0)).astype(BF16)
    by_row = spread_of(iota((128, 128), 0), iota((128, 128), 1)).astype(BF16)
    WF[...] = dot(WS[...].reshape(C, 128).astype(BF16), by_col).astype(BF16)
    WI[...] = dot(by_row, Win[...].astype(BF16)).astype(BF16)
    valid = iota((TOK, 128), 0) // COLS == (iota((TOK, 128), 1) % 8) // 2

    real = iota((1, 128), 1) < CTX_TOK

    def spread(act, at, n):
        col = iota((n, C), 0) % COLS
        rows = pl.ds(at, n)
        A[rows, C : 2 * C] = act.astype(BF16)
        A[rows, 0:C] = jnp.where(col == 0, 0.0, pltpu.roll(act, 1, 0)).astype(BF16)
        A[rows, 2 * C : 3 * C] = jnp.where(col == COLS - 1, 0.0, pltpu.roll(act, n - 1, 0)).astype(BF16)

    def denoise(t, carry):
        scale = choose(t, [p[0] for p in PLANS])
        beta = choose(t, [p[1] for p in PLANS])
        sigma = choose(t, [p[2] for p in PLANS])
        weight = choose(t, [p[1] / p[2] for p in PLANS])
        bias = bias_ref[pl.ds(t, 1), :]
        w_first = WI[...]
        hidden = dot(PB[t, COLS : COLS + TOK, :], w_first) + bias
        spread(silu(rms(hidden, g1_ref[...].reshape(1, C))), COLS, TOK)
        M[...] = hidden + dot(A[COLS : COLS + TOK, :], Wc[3 * C : 6 * C, :])
        M[COLS:TOK, :] += dot(A[COLS:TOK, :], Wc[0 : 3 * C, :])
        wait_halo(t)
        edge = jnp.concatenate([PB[t, 0:COLS, :], PB[t, COLS + TOK :, :]], axis=0)
        act = silu(rms(dot(edge, w_first) + bias, g1_ref[...].reshape(1, C)))
        above = jnp.where(pos > 0, act[0:COLS], 0.0)
        below = jnp.where(pos < 15, act[COLS:], 0.0)
        spread(above, 0, COLS)
        spread(below, COLS + TOK, COLS)
        M[0:COLS, :] += dot(A[0:COLS, :], Wc[0 : 3 * C, :])
        M[...] += dot(A[2 * COLS :, :], Wc[6 * C : 9 * C, :])

        mixed = M[...]
        normed = rms(mixed, g2_ref[...].reshape(1, C)).astype(BF16)
        queries = dot(normed, Wq[...]).astype(BF16)
        heads = []
        for p in range(PAIRS):
            e = jnp.exp(dot(queries[:, 128 * p : 128 * (p + 1)], Kbd[p]))
            shares = []
            for half in (e[:, 0:128], e[:, 128:256]):
                total = jnp.sum(jnp.where(real, half, 0.0), axis=1, keepdims=True)
                shares.append(half * (1.0 / total))
            heads.append(dot(jnp.concatenate(shares, axis=1).astype(BF16), Vbd[p]).astype(BF16))
        out = mixed + dot(jnp.concatenate(heads, axis=1), Wo[...])

        def finish(ranges):
            def part(v):
                return jnp.concatenate([v[a:b] for a, b in ranges], axis=0)

            def load(ref, *lead):
                return jnp.concatenate([ref[(*lead, slice(a, b))] for a, b in ranges], axis=0)

            final = silu(rms(part(out), g3_ref[...].reshape(1, C))).astype(BF16)
            predicted = jnp.where(part(valid), dot(final, WF[...]), 0.0)
            x_new = scale * load(X) + beta * predicted + sigma * load(NZT, t)
            at = 0
            for a, b in ranges:
                n = b - a
                FA[a:b, :] = final[at : at + n]
                X[a:b, :] = x_new[at : at + n]
                PB[t + 1, a + COLS : b + COLS, :] = x_new[at : at + n].astype(BF16)
                at += n

        finish(((0, COLS), (TOK - COLS, TOK)))

        @pl.when(t < STEPS - 1)
        def _():
            start_halo(t + 1)

        finish(((COLS, TOK - COLS),))
        GA[...] += weight * dot(NTS[t], FA[...])
        return carry

    table = jnp.concatenate([KG[s, 80:88, :].astype(F32)[0:1] for s in range(16)], axis=0)
    ids = table[:, 0:1]
    rewards = table[:, 1:2] + table[:, 2:3] + table[:, 3:4]
    here = iota((16, 1), 0) == image
    own_id = jnp.sum(jnp.where(here, ids, 0.0), axis=0, keepdims=True)
    own_reward = jnp.sum(jnp.where(here, rewards, 0.0), axis=0, keepdims=True)
    same = jnp.where(ids == own_id, 1.0, 0.0)
    count = jnp.maximum(jnp.sum(same, axis=0, keepdims=True), 1.0)
    mean = jnp.sum(same * rewards, axis=0, keepdims=True) / count
    square = jnp.sum(same * (rewards * rewards), axis=0, keepdims=True) / count
    spread_1 = jnp.sqrt(jnp.maximum(square - mean * mean, 1.0))
    advantage = (own_reward - mean) / spread_1

    lax.fori_loop(0, STEPS, denoise, 0)

    lane128 = iota((FEAT, 128), 1)
    fold = spread_of(lane128 % 64, iota((FEAT, 128), 0)).astype(BF16)
    grad = sum(dot(fold, part) for part in split(GA[...])) * (advantage * (-1.0 / 16.0))
    for j in range(5):
        GS[:, j, :] = grad[:, 128 * j : 128 * (j + 1)]

    def column_copy(k):
        peer = lax.rem(dev + k, 16)
        return to_peer(GS.at[peer], GR.at[dev], r_send.at[k], r_recv.at[k], (sec, peer))

    for k in range(1, 16):
        column_copy(k).start()
    GR[dev] = GS[dev]
    flat = X[0:COLS, 0:64]
    for r in range(1, ROWS):
        flat = flat + X[r * COLS : (r + 1) * COLS, 0:64]
    flat = jnp.concatenate([flat[:, 0:32], flat[:, 32:64]], axis=0)
    XO[0] = sum(
        lax.dot_general(part, pick, (((0,), (0,)), ((), ())), preferred_element_type=F32) for part in split(flat)
    )

    @pl.when(jnp.logical_not(stays))
    def _():
        latents_out().start()

    for k in range(1, 16):
        column_copy(k).wait()
    R1[...] = jnp.sum(GR[...], axis=0)

    def row_copy(k):
        return to_peer(R1, RR.at[sec], s_send.at[k], s_recv.at[k], (lax.rem(sec + k, 16), dev))

    for k in range(1, 16):
        row_copy(k).start()
    RR[sec] = R1[...]
    for k in range(1, 16):
        row_copy(k).wait()
    total = jnp.sum(RR[...], axis=0)
    picked = jnp.zeros((128, 128), F32)
    want = iota((128, 128), 0) + sec * SHARD
    for j in range(5):
        hit = iota((128, 128), 1) + 128 * j == want
        picked = jnp.where(hit, jnp.broadcast_to(total[j : j + 1], (128, 128)), picked)
    @pl.when(jnp.logical_not(stays))
    def _():
        latents_out().wait()
        x_out[...] = XO[1]

    @pl.when(stays)
    def _():
        x_out[...] = XO[0]

    g_out[...] = jnp.sum(jnp.transpose(picked), axis=0, keepdims=True)[:, 0:SHARD]


def per_device(
    latents,
    noise,
    rewards,
    prompt_ids,
    context,
    time_bias,
    gain_first,
    gain_second,
    gain_third,
    w_in,
    w_conv,
    w_query,
    w_key,
    w_value,
    w_attn_out,
    w_final,
    moment_first,
    moment_second,
):
    words, width = context.shape[1:]
    flat_context = context.transpose(1, 0, 2).reshape(words * context.shape[0], width)
    vmem = pl.BlockSpec(memory_space=pltpu.VMEM)
    dma = pltpu.SemaphoreType.DMA
    x_new, grad = pl.pallas_call(
        body,
        out_shape=(jax.ShapeDtypeStruct((32, 128), F32), jax.ShapeDtypeStruct((1, SHARD), F32)),
        in_specs=[vmem] * 4 + [pl.BlockSpec(memory_space=pl.ANY)] + [vmem] * 11,
        out_specs=(vmem,) * 2,
        scratch_shapes=[
            pltpu.VMEM(flat_context.shape, BF16),
            pltpu.VMEM((32 * (STEPS + 1), 128), F32),
            pltpu.VMEM((2, 32, 128), F32),
            pltpu.VMEM((88, 128), BF16),
            pltpu.VMEM((NZ, 2, NX, 2, 2, SHARD, LANES), BF16),
            pltpu.VMEM((16, 88, 128), BF16),
            pltpu.VMEM((16, 80, 128), BF16),
            pltpu.VMEM((9 * C, C), BF16),
            pltpu.VMEM((C, C), BF16),
            pltpu.VMEM((C, C), BF16),
            pltpu.VMEM((128, C), F32),
            pltpu.VMEM((NZ, 2, SHARD, 128), F32),
            pltpu.VMEM((C, 128), BF16),
            pltpu.VMEM((128, C), BF16),
            pltpu.VMEM((PAIRS, 128, 256), BF16),
            pltpu.VMEM((PAIRS, 256, 128), BF16),
            pltpu.VMEM((STEPS + 1, TOK + 2 * COLS, 128), BF16),
            pltpu.VMEM((TOK + 2 * COLS, 3 * C), BF16),
            pltpu.VMEM((TOK, C), F32),
            pltpu.VMEM((TOK, 128), F32),
            pltpu.VMEM((STEPS, TOK, 128), F32),
            pltpu.VMEM((STEPS, 128, TOK), BF16),
            pltpu.VMEM((TOK, C), BF16),
            pltpu.VMEM((128, C), F32),
            pltpu.VMEM((16, 8, 128), F32),
            pltpu.VMEM((16, 8, 128), F32),
            pltpu.VMEM((8, 128), F32),
            pltpu.VMEM((16, 8, 128), F32),
            dma((3, 8)),
            dma((3, 8)),
            dma((3, 4)),
            dma((3, 4)),
            dma((3, 4, 2, 4)),
            dma((3, 4, 2, 4)),
            dma((28,)),
            dma((28,)),
            dma((16,)),
            dma((16,)),
            dma((16,)),
            dma((16,)),
            dma((STEPS, 2)),
            dma((STEPS, 2)),
            dma((16,)),
            dma((16,)),
            dma((16,)),
            dma((16,)),
            dma((3,)),
            dma((3,)),
            dma,
        ],
        compiler_params=pltpu.CompilerParams(
            collective_id=0, has_side_effects=True, vmem_limit_bytes=58 * 1024 * 1024
        ),
        name="ddpo",
    )(
        latents.reshape(32, 128),
        noise.reshape(STEPS * 32, 128),
        rewards.reshape(1, 1),
        prompt_ids.reshape(1, 1),
        flat_context,
        time_bias,
        gain_first,
        gain_second,
        gain_third,
        w_in,
        w_conv.T,
        w_query,
        w_key.T,
        w_value.T,
        w_attn_out,
        w_final.T,
    )
    g = grad.T
    moment_one = 0.9 * moment_first + 0.1 * g
    moment_two = 0.999 * moment_second + 0.001 * g * g
    new_weight = w_final - learn_rate * moment_one / (jnp.sqrt(moment_two) + 1e-08)
    return (x_new.reshape(latents.shape), new_weight, moment_one, moment_two)


def solution(mesh):
    placed = (
        P("sec", None, "dev", None),
        P(None, "sec", None, "dev", None),
        P("sec"),
        P("sec"),
        P(),
        P(),
        P(),
        P(),
        P(),
        P("sec", "dev"),
        P("sec", "dev"),
        P("sec", "dev"),
        P("sec", "dev"),
        P("sec", "dev"),
        P("sec", "dev"),
        P("sec", "dev"),
        P("sec", "dev"),
        P("sec", "dev"),
    )
    return jax.shard_map(
        per_device,
        mesh=mesh,
        in_specs=placed,
        out_specs=(P("sec", None, "dev", None), P("sec", "dev"), P("sec", "dev"), P("sec", "dev")),
        check_vma=False,
    )
```
